256 devices in a mesh: tm: 32 (over y, x, core), height: 8 (over z).
Axes of the slice: x: 4, y: 4, z: 8, core: 2. Of those that a mesh axis runs over, the one named last changes fastest.
Arguments:
- latent: bfloat16 [64, 32, 80, 256], P('tm', 'height'), may hold values from -64 to 64, as said below
- target: bfloat16 [64, 32, 80, 256], P('tm', 'height'), may hold values from -6 to 6
- conv_weight: bfloat16 [3, 3, 3, 256, 256], replicated, may hold values from -0.078125 to 0.078125
- group_norm_gain: float32 [256], replicated, may hold values from 0.1 to 1.9
- group_norm_bias: float32 [256], replicated, may hold values from -3 to 3
Outputs:
- decoded: bfloat16 [64, 32, 80, 256], P('tm', 'height')
- grad_latent: bfloat16 [64, 32, 80, 256], P('tm', 'height')
- weight_grad: float32 [3, 3, 3, 256, 256], P(None, None, None, None, 'height')
- norm_gain_gradient: float32 [256], replicated
- bias_grad: float32 [256], replicated
The draws below stay inside these ranges and needn't reach their ends.
Inputs may be any that keep to these rules, and one draw needn't show every extreme that they name: `latent`: finite feature values.
All inputs are finite; a program needn't handle non-finite values.
Results may differ from the reference program's by a relative error of at most 0.0015.
The reference program's roundings to bfloat16 on the way (of `act` and `grad_half`) count: a program that leaves them out, or rounds other values in their place, can miss the bound.
Values may be sent and summed in bfloat16 or wider, within the bound.
A program may use at most 128 MiB of HBM per device.

```python
import jax
import jax.numpy as jnp
from jax import lax

FEATURE_CHANNELS = 256
NORM_GROUPS = 32
WIDTH = 80
FRAMES = 64
ROWS = 32


def draw_latent(key, part):
    key_base = jax.random.fold_in(key, 11)
    key_chan = jax.random.fold_in(key, 12)
    key_off = jax.random.fold_in(key, 13)
    tpos = jnp.arange(FRAMES, dtype=jnp.float32) / (FRAMES - 1)
    rpos = jnp.arange(ROWS, dtype=jnp.float32) / (ROWS - 1)
    ramp = jnp.sqrt((1.0 + 2.0 * tpos)[:, None] * (1.0 + 2.0 * rpos)[None, :])[:, :, None, None]
    chan = jnp.exp(jax.random.uniform(key_chan, (FEATURE_CHANNELS,), jnp.float32, -1.0, 1.0))
    base = jnp.clip(jax.random.normal(key_base, (FRAMES, ROWS, WIDTH, FEATURE_CHANNELS), jnp.float32), -6.0, 6.0)
    offset = jax.random.uniform(key_off, (FEATURE_CHANNELS,), jnp.float32, 0.3, 1.0)[None, None, None, :]
    return ((base + offset) * ramp * chan).astype(jnp.bfloat16)


def with_spikes(array, stream_key, source, target, blocks, factor):
    def block_of(dim):
        return (jnp.arange(array.shape[dim]) // (array.shape[dim] // blocks)).reshape((-1,) + (1,) * (array.ndim - 1 - dim))

    one_side = jax.random.permutation(stream_key, blocks)[block_of(target)]
    other_side = (block_of(target) + blocks // 2) % blocks
    return jnp.where((block_of(source) == one_side) | (block_of(source) == other_side), factor * array, array)


def steps_of(key, dims, cuts, least, high):
    loudness = 1.0
    for position, shards_of in cuts:
        heights = jax.random.uniform(jax.random.fold_in(jax.random.fold_in(key, 6), position), (shards_of,), jnp.float32, least / len(cuts), high / len(cuts))
        loudness = loudness * jnp.repeat(jnp.exp(heights), dims[position] // shards_of).reshape((-1,) + (1,) * (len(dims) - 1 - position))
    return loudness


def bell_draw(stream_key, extent, width, bound, cuts=(), held_as=jnp.bfloat16):
    values = width * jax.random.normal(stream_key, extent, jnp.float32)
    if cuts:
        values = values * steps_of(stream_key, extent, cuts, -0.22, 0.18)
    return jnp.clip(values, -bound, bound).astype(held_as)


def heavy_noise(stream_key, dims, deviation, limit, pieces, heavy, held_as=jnp.bfloat16):
    result = deviation * jax.random.normal(stream_key, dims, jnp.float32)
    if pieces:
        result = result * steps_of(stream_key, dims, pieces, -0.22, 0.18)
    return jnp.clip(with_spikes(result, jax.random.fold_in(stream_key, 3), *heavy), -limit, limit).astype(held_as)


def setup_inputs(seed: int = 0) -> dict:
    key_of = jax.random.split(jax.random.key(seed), 6)
    latent = draw_latent(jax.random.fold_in(key_of[5], 71), 0)
    target = heavy_noise(key_of[1], (FRAMES, ROWS, WIDTH, FEATURE_CHANNELS), 1.0, 6.0, ((0, 32), (1, 8)), (0, 3, 32, 2.75))
    conv_weight = bell_draw(key_of[2], (3, 3, 3, FEATURE_CHANNELS, FEATURE_CHANNELS), (27 * FEATURE_CHANNELS) ** -0.5, 0.078125)
    group_norm_gain = jnp.clip(1.0 + 0.18 * jax.random.normal(key_of[3], (FEATURE_CHANNELS,), jnp.float32), 0.1, 1.9)
    group_norm_bias = bell_draw(key_of[4], (FEATURE_CHANNELS,), 0.5, 3.0, (), jnp.float32)
    return dict(latent=latent, target=target, conv_weight=conv_weight, group_norm_gain=group_norm_gain, group_norm_bias=group_norm_bias)


EPS = 1e-06

def reference(latent, target, conv_weight, group_norm_gain, group_norm_bias):
    channels_per_group = FEATURE_CHANNELS // NORM_GROUPS
    x32 = latent.astype(jnp.float32).reshape(-1, FEATURE_CHANNELS)
    group_view = x32.reshape(-1, NORM_GROUPS, channels_per_group)
    group_average = lax.optimization_barrier(jnp.mean(group_view, axis=(0, 2)))
    spread = lax.optimization_barrier(jnp.mean(jnp.square(group_view - group_average[None, :, None]), axis=(0, 2)))
    inverse_deviation = lax.rsqrt(spread + EPS)
    normalized_input = ((group_view - group_average[None, :, None]) * inverse_deviation[None, :, None]).reshape(-1, FEATURE_CHANNELS)
    preact_values = normalized_input * group_norm_gain + group_norm_bias
    act = jax.nn.silu(preact_values).astype(jnp.bfloat16).reshape(FRAMES, ROWS, WIDTH, FEATURE_CHANNELS)
    apad = jnp.pad(act, ((2, 0), (1, 1), (1, 1), (0, 0)))
    conv = jnp.zeros((FRAMES * ROWS * WIDTH, FEATURE_CHANNELS), jnp.float32)
    for kt in range(3):
        for kr in range(3):
            for kc in range(3):
                piece = apad[kt:kt + FRAMES, kr:kr + ROWS, kc:kc + WIDTH].reshape(-1, FEATURE_CHANNELS)
                conv = conv + jnp.dot(piece, conv_weight[kt, kr, kc], preferred_element_type=jnp.float32)
    out = x32 + conv
    decoded = out.astype(jnp.bfloat16).reshape(FRAMES, ROWS, WIDTH, FEATURE_CHANNELS)
    output_gradient = out - target.astype(jnp.float32).reshape(-1, FEATURE_CHANNELS)
    grad_half = output_gradient.astype(jnp.bfloat16)
    gpad = jnp.pad(grad_half.reshape(FRAMES, ROWS, WIDTH, FEATURE_CHANNELS), ((0, 2), (1, 1), (1, 1), (0, 0)))
    back = jnp.zeros((FRAMES * ROWS * WIDTH, FEATURE_CHANNELS), jnp.float32)
    taps = []
    for kt in range(3):
        for kr in range(3):
            for kc in range(3):
                piece = apad[kt:kt + FRAMES, kr:kr + ROWS, kc:kc + WIDTH].reshape(-1, FEATURE_CHANNELS)
                taps.append(lax.dot_general(piece, grad_half, (((0,), (0,)), ((), ())), preferred_element_type=jnp.float32))
                gpiece = gpad[2 - kt:2 - kt + FRAMES, 2 - kr:2 - kr + ROWS, 2 - kc:2 - kc + WIDTH].reshape(-1, FEATURE_CHANNELS)
                back = back + jnp.dot(gpiece, conv_weight[kt, kr, kc].T, preferred_element_type=jnp.float32)
    weight_grad = jnp.stack(taps).reshape(3, 3, 3, FEATURE_CHANNELS, FEATURE_CHANNELS)
    sig = jax.nn.sigmoid(preact_values)
    preact_gradient = back * sig * (1.0 + preact_values * (1.0 - sig))
    norm_gain_gradient = lax.optimization_barrier(jnp.sum(preact_gradient * normalized_input, axis=0))
    bias_grad = lax.optimization_barrier(jnp.sum(preact_gradient, axis=0))
    normalized_gradient = preact_gradient * group_norm_gain
    first_moment = lax.optimization_barrier(jnp.mean(normalized_gradient.reshape(-1, NORM_GROUPS, channels_per_group), axis=(0, 2)))
    second_moment = lax.optimization_barrier(jnp.mean((normalized_gradient * normalized_input).reshape(-1, NORM_GROUPS, channels_per_group), axis=(0, 2)))
    channel_inverse_deviation = jnp.repeat(inverse_deviation, channels_per_group)
    input_gradient = output_gradient + channel_inverse_deviation * (normalized_gradient - jnp.repeat(first_moment, channels_per_group) - normalized_input * jnp.repeat(second_moment, channels_per_group))
    grad_latent = input_gradient.astype(jnp.bfloat16).reshape(FRAMES, ROWS, WIDTH, FEATURE_CHANNELS)
    return (decoded, grad_latent, weight_grad, norm_gain_gradient, bias_grad)
```

```python
import functools

import jax
import jax.numpy as jnp
from jax import lax
from jax.experimental import pallas as pl
from jax.experimental.pallas import tpu as pltpu
from jax.sharding import PartitionSpec as P

NORM_GROUPS = 32
EPS = 1e-06
MESH = pl.DeviceIdType.MESH
F32 = jnp.float32
BF16 = jnp.bfloat16
UA = 5
UB = 4


def group_sum(v):
    lane = lax.broadcasted_iota(jnp.int32, v.shape, 1)
    width = v.shape[1]
    for k in (1, 2, 4):
        other = jnp.where(
            lax.rem(lax.div(lane, k), 2) == 1,
            pltpu.roll(v, k, 1),
            pltpu.roll(v, width - k, 1),
        )
        v = v + other
    return v


def pack(a, b):
    half = a.shape[1] // 2
    return jnp.concatenate(
        [a[:, :half], a[:, half:], b[:, :half], b[:, half:], jnp.zeros((4, half), F32)], axis=0
    )


def unpack(v):
    a = jnp.concatenate([v[0:1], v[1:2]], axis=1)
    b = jnp.concatenate([v[2:3], v[3:4]], axis=1)
    return a, b


def kernel(
    nx, ny, nz, cells,
    latent, target_hbm, w_hbm, gain_ref, bias_ref,
    decoded, grad_latent, wgrad, ngrad, bgrad,
    L, A, G, graw, g32, acc, W, WT, target, gta, gtb,
    DA, DB, RCA, RCB,
    axp, axm, axf, azp, azm, azf, bzp, bzm, bzf, bxp, bxm, bxf,
    YB, XG, AR,
    in_sem, lat_s, lat_r, gh_s, gh_r, ar_s, ar_r, co_s, co_r,
    ring_s, ring_r, y_s, y_r, xg_s, xg_r, cg_s, cg_r,
):
    t = lax.axis_index("tm")
    z = lax.axis_index("height")
    nt = 2 * nx * ny
    core = lax.rem(t, 2)
    x = lax.rem(lax.div(t, 2), nx)
    y = lax.div(t, 2 * nx)
    frames, rows, width, ch = latent.shape

    def at(yy, xx, cc):
        return (yy * nx + xx) * 2 + cc

    def remote(src, dst, ss, rs, tt, zz):
        return pltpu.make_async_remote_copy(
            src_ref=src, dst_ref=dst, send_sem=ss, recv_sem=rs,
            device_id=(tt, zz), device_id_type=MESH,
        )

    up_t, dn_t = lax.rem(t + 1, nt), lax.rem(t + nt - 1, nt)
    up_z, dn_z = lax.rem(z + 1, nz), lax.rem(z + nz - 1, nz)
    up_x, dn_x = lax.rem(x + 1, nx), lax.rem(x + nx - 1, nx)

    n1, n2 = 2 * nz, nx * ny
    me1, me2 = core * nz + z, y * nx + x

    def peer1(k):
        p = lax.rem(me1 + k, n1)
        return at(y, x, lax.div(p, nz)), lax.rem(p, nz)

    def peer2(k):
        p = lax.rem(me2 + k, n2)
        return p * 2 + core, z

    barrier = pltpu.get_barrier_semaphore()

    def greet(tt, zz):
        pl.semaphore_signal(barrier, inc=1, device_id=(tt, zz), device_id_type=MESH)

    def greet1(k, c):
        greet(*peer1(k))
        return c

    def greet2(k, c):
        greet(*peer2(k))
        return c

    lax.fori_loop(1, n1, greet1, 0)
    lax.fori_loop(1, n2, greet2, 0)
    for tt in (up_t, dn_t):
        for zz in (dn_z, z, up_z):
            greet(tt, zz)

    weights_in = pltpu.make_async_copy(w_hbm, W, in_sem.at[0])
    target_in = pltpu.make_async_copy(target_hbm, target, in_sem.at[1])
    weights_in.start()
    target_in.start()

    def sum_rows(i, total):
        v = latent[lax.div(i, rows), lax.rem(i, rows)].astype(F32)
        return total + jnp.sum(v.reshape(width // 8, 8, ch), axis=0)

    count = frames * rows * width * 8
    total = lax.fori_loop(0, frames * rows, sum_rows, jnp.zeros((8, ch), F32))
    mean_l = group_sum(jnp.sum(total, axis=0, keepdims=True)) / count

    def sum_squares(i, total):
        v = latent[lax.div(i, rows), lax.rem(i, rows)].astype(F32) - mean_l
        return total + jnp.sum((v * v).reshape(width // 8, 8, ch), axis=0)

    total = lax.fori_loop(0, frames * rows, sum_squares, jnp.zeros((8, ch), F32))
    sq_l = group_sum(jnp.sum(total, axis=0, keepdims=True))

    pl.semaphore_wait(barrier, (n1 - 1) + (n2 - 1) + 6)

    def spread_out(stage, value):
        me, n, peer = (me1, n1, peer1) if stage % 2 == 0 else (me2, n2, peer2)
        slots = AR.at[stage]
        AR[stage, me] = value

        def send(k, c):
            tt, zz = peer(k)
            remote(slots.at[me], slots.at[me], ar_s.at[stage, k], ar_r.at[stage, k], tt, zz).start()
            return c

        lax.fori_loop(1, n, send, 0)

    def gather_in(stage):
        me, n, peer = (me1, n1, peer1) if stage % 2 == 0 else (me2, n2, peer2)
        slots = AR.at[stage]

        def arrive(k, c):
            tt, zz = peer(k)
            remote(slots.at[me], slots.at[me], ar_s.at[stage, k], ar_r.at[stage, k], tt, zz).wait()
            return c

        lax.fori_loop(1, n, arrive, 0)
        return n

    def plain_total(stage, n):
        total = AR[stage, 0]
        for k in range(1, n):
            total = total + AR[stage, k]
        return total

    def moments(stage, n, members):
        mean = plain_total(stage, n) / n
        row = lax.broadcasted_iota(jnp.int32, mean.shape, 0)
        mean = mean[0:2]
        sq = jnp.zeros_like(mean)
        for k in range(n):
            d = AR[stage, k, 0:2] - mean
            sq = sq + (AR[stage, k, 2:4] + (d * d) * members)
        del row
        return jnp.concatenate([mean, sq, jnp.zeros((4, mean.shape[1]), F32)], axis=0)

    spread_out(0, pack(mean_l, sq_l))

    def halo(block, buf, first, other, tt, ss, rs):
        edge0, edge1 = block.at[:, 0], block.at[:, rows - 1]
        mine, theirs = pl.ds(first, frames), pl.ds(other, frames)
        return [
            remote(block, buf.at[theirs, pl.ds(1, rows)], ss.at[0], rs.at[0], tt, z),
            remote(edge1, buf.at[mine, 0], ss.at[1], rs.at[1], t, up_z),
            remote(edge0, buf.at[mine, rows + 1], ss.at[2], rs.at[2], t, dn_z),
            remote(edge1, buf.at[theirs, 0], ss.at[3], rs.at[3], tt, up_z),
            remote(edge0, buf.at[theirs, rows + 1], ss.at[4], rs.at[4], tt, dn_z),
        ]

    lat_halo = halo(latent, L, frames, 0, up_t, lat_s, lat_r)
    for c in lat_halo:
        c.start()
    for f in range(frames):
        for r in range(rows):
            L[frames + f, 1 + r] = latent[f, r]

    weights_in.wait()

    def flip(u, c):
        for kc in range(3):
            WT[8 - u, (2 - kc) * ch : (3 - kc) * ch, :] = W[u, kc * ch : (kc + 1) * ch, :].T
        return c

    n = gather_in(0)
    level = moments(0, n, count)
    spread_out(1, level)
    lax.fori_loop(0, 9, flip, 0)
    n = gather_in(1)
    mean, sq = unpack(moments(1, n, count * n1))
    everything = count * n1 * n2
    rstd = lax.rsqrt(sq / everything + EPS)
    gain, bias = gain_ref[...], bias_ref[...]
    scale = rstd * gain

    for c in lat_halo:
        c.wait()

    col = lax.broadcasted_iota(jnp.int32, (width, ch), 0)

    def store_shifts(buf, f, r, v):
        buf[f, r, :, 0:ch] = jnp.where(col == 0, 0.0, pltpu.roll(v, 1, 0)).astype(BF16)
        buf[f, r, :, ch : 2 * ch] = v.astype(BF16)
        buf[f, r, :, 2 * ch : 3 * ch] = jnp.where(
            col == width - 1, 0.0, pltpu.roll(v, width - 1, 0)
        ).astype(BF16)

    def inside(f, r, lone, edge):
        top = jnp.logical_or(r > 0, z > 0)
        low = jnp.logical_or(r < rows + 1, z < nz - 1)
        return jnp.logical_and(jnp.logical_or(lone, edge), jnp.logical_and(top, low))

    def activate(i, c):
        f, r = lax.div(i, rows + 2), lax.rem(i, rows + 2)
        zz = (L[f, r].astype(F32) - mean) * scale + bias
        v = zz / (1.0 + jnp.exp(-zz))
        keep = inside(f, r, f >= frames, t > 0)
        store_shifts(A, f, r, jnp.where(keep, v, 0.0))
        return c

    lax.fori_loop(0, 2 * frames * (rows + 2), activate, 0)

    size = frames * rows * width

    def piece(buf, u):
        kt, kr = lax.div(u, 3), lax.rem(u, 3)
        return buf[pl.ds(kt, frames), pl.ds(kr, rows)].reshape(size, 3 * ch)

    def conv(buf, w):
        acc[...] = jnp.dot(piece(buf, 0), w[0], preferred_element_type=F32)

        def tap(u, c):
            acc[...] += jnp.dot(piece(buf, u), w[u], preferred_element_type=F32)
            return c

        lax.fori_loop(1, 9, tap, 0)

    conv(A, W)
    target_in.wait()

    def finish(i, c):
        f, r = lax.div(i, rows), lax.rem(i, rows)
        at_row = pl.ds(pl.multiple_of(i * width, 16), width)
        out = latent[f, r].astype(F32) + acc[at_row, :]
        decoded[f, r] = out.astype(BF16)
        g = out - target[f, r].astype(F32)
        g32[at_row, :] = g
        graw[f, 1 + r] = g.astype(BF16)
        return c

    lax.fori_loop(0, frames * rows, finish, 0)

    own = graw.at[pl.ds(0, frames), pl.ds(1, rows)]
    g_halo = halo(own, graw, 0, frames, dn_t, gh_s, gh_r)
    for c in g_halo:
        c.start()

    per = ch // (nx * nz)
    for b in range(ch // 128):
        for s in range(size // 128):
            gtb[b * 128 : (b + 1) * 128, s * 128 : (s + 1) * 128] = (
                g32[s * 128 : (s + 1) * 128, b * 128 : (b + 1) * 128].T
            )
    for zz in range(nz):
        for xx in range(nx):
            gta[(xx * nz + zz) * per : (xx * nz + zz + 1) * per] = (
                gtb[(zz * nx + xx) * per : (zz * nx + xx + 1) * per]
            )

    other = 1 - core

    def to_sibling_a(u):
        return remote(DA.at[other, u], RCA.at[u], co_s.at[u], co_r.at[u], at(y, x, other), z)

    def to_sibling_b(u):
        return remote(
            DB.at[other, u], RCB.at[u], co_s.at[UA + u], co_r.at[UA + u], at(y, x, other), z
        )

    half = ch // 2

    def kernel_term(gt, D, unit, u):
        res = jnp.dot(gt[...].astype(BF16), piece(A, unit), preferred_element_type=F32)
        d = D.shape
        for kc in range(3):
            for h in range(2):
                lo = kc * ch + h * half
                D[h, u, :, :, kc] = res[:, lo : lo + half].reshape(d[2], d[3], per, half)

    def term_a(u, c):
        kernel_term(gta, DA, u, u)
        to_sibling_a(u).start()
        return c

    def term_b(u, c):
        kernel_term(gtb, DB, UA + u, u)
        to_sibling_b(u).start()
        return c

    lax.fori_loop(0, UB, term_b, 0)
    lax.fori_loop(0, UA, term_a, 0)

    class Ring:
        def __init__(self, n, me, up, down, chunk, cut, first, second, full, unit, step0):
            self.n, self.me, self.up, self.down = n, me, up, down
            self.chunk, self.cut = chunk, cut
            self.first, self.second, self.full = first, second, full
            self.unit, self.step0 = unit, step0
            self.steps = n // 2

        def sends(self, u, s):
            n, me, k, i = self.n, self.me, self.unit(u), self.step0 + s
            sems = [(ring_s.at[k, i, d], ring_r.at[k, i, d]) for d in range(2)]
            if s == 0:
                c = self.chunk(u, lax.rem(me + n // 2, n))
                size_ = c.shape[0]
                src = [c.at[pl.ds(0, self.cut)], c.at[pl.ds(self.cut, size_ - self.cut)]]
                dst = [self.first.at[u], self.second.at[u]]
            else:
                src = [
                    self.chunk(u, lax.rem(me + n // 2 - s, n)),
                    self.chunk(u, lax.rem(me + n - n // 2 + s, n)),
                ]
                dst = [self.full.at[u, s - 1, 0], self.full.at[u, s - 1, 1]]
            return [
                remote(src[0], dst[0], *sems[0], *self.up),
                remote(src[1], dst[1], *sems[1], *self.down),
            ]

        def send(self, u, s):
            for c in self.sends(u, s):
                c.start()

        def receive(self, u, s):
            n, me = self.n, self.me
            for c in self.sends(u, s):
                c.wait_recv()
            left = self.chunk(u, lax.rem(me + n - 1 + n // 2 - s, n))
            right = self.chunk(u, lax.rem(me + n + 1 - n // 2 + s, n))
            if s == 0:
                size_ = left.shape[0]
                head, tail = pl.ds(0, self.cut), pl.ds(self.cut, size_ - self.cut)
                left[head] = left[head] + self.first[u]
                right[tail] = right[tail] + self.second[u]
            else:
                left[...] = left[...] + self.full[u, s - 1, 0]
                right[...] = right[...] + self.full[u, s - 1, 1]

        def sent(self, u, s):
            for c in self.sends(u, s):
                c.wait_send()

    x_up, x_down = (at(y, up_x, core), z), (at(y, dn_x, core), z)
    z_up, z_down = (t, up_z), (t, dn_z)
    sx, sz = nx // 2, nz // 2
    a_unit = lambda u: u
    b_unit = lambda u: UA + u
    ring_ax = Ring(
        nx, x, x_up, x_down, lambda u, c: DA.at[core, u, c], nz // 2, axp, axm, axf, a_unit, 0
    )
    ring_az = Ring(
        nz, z, z_up, z_down, lambda u, c: DA.at[core, u, x, c], 2, azp, azm, azf, a_unit, sx
    )
    ring_bz = Ring(
        nz, z, z_up, z_down, lambda u, c: DB.at[core, u, c], nx // 2, bzp, bzm, bzf, b_unit, 0
    )
    ring_bx = Ring(
        nx, x, x_up, x_down, lambda u, c: DB.at[core, u, z, c], 2, bxp, bxm, bxf, b_unit, sz
    )
    plan_a = [(ring_ax, s) for s in range(sx)] + [(ring_az, s) for s in range(sz)]
    plan_b = [(ring_bz, s) for s in range(sz)] + [(ring_bx, s) for s in range(sx)]

    def first_a(u, c):
        to_sibling_a(u).wait_recv()
        DA[core, u] = DA[core, u] + RCA[u]
        plan_a[0][0].send(u, 0)
        return c

    def first_b(u, c):
        to_sibling_b(u).wait_recv()
        DB[core, u] = DB[core, u] + RCB[u]
        plan_b[0][0].send(u, 0)
        return c

    lax.fori_loop(0, UB, first_b, 0)
    lax.fori_loop(0, UA, first_a, 0)

    def wave(w):
        def go(plan, u):
            ring, s = plan[w]
            ring.receive(u, s)
            if w + 1 < len(plan):
                ring, s = plan[w + 1]
                ring.send(u, s)

        def go_a(u, c):
            go(plan_a, u)
            return c

        def go_b(u, c):
            go(plan_b, u)
            return c

        lax.fori_loop(0, UB, go_b, 0)
        lax.fori_loop(0, UA, go_a, 0)

    for c in g_halo:
        c.wait()

    def shift_gradient(i, c):
        f, r = lax.div(i, rows + 2), lax.rem(i, rows + 2)
        keep = inside(f, r, f < frames, t < nt - 1)
        store_shifts(G, f, r, jnp.where(keep, graw[f, r].astype(F32), 0.0))
        return c

    lax.fori_loop(0, 2 * frames * (rows + 2), shift_gradient, 0)
    wave(0)
    conv(G, WT)

    def through_norm(i, carry):
        s0, s1 = carry
        f, r = lax.div(i, rows), lax.rem(i, rows)
        at_row = pl.ds(pl.multiple_of(i * width, 16), width)
        d = latent[f, r].astype(F32) - mean
        zz = d * scale + bias
        sig = 1.0 / (1.0 + jnp.exp(-zz))
        gz = acc[at_row, :] * sig * (1.0 + zz * (1.0 - sig))
        acc[at_row, :] = gz
        xhat = d * rstd
        s0 = s0 + jnp.sum(gz.reshape(width // 8, 8, ch), axis=0)
        s1 = s1 + jnp.sum((gz * xhat).reshape(width // 8, 8, ch), axis=0)
        return s0, s1

    zero = jnp.zeros((8, ch), F32)
    s0, s1 = lax.fori_loop(0, frames * rows, through_norm, (zero, zero))
    spread_out(2, pack(jnp.sum(s0, axis=0, keepdims=True), jnp.sum(s1, axis=0, keepdims=True)))
    last = len(plan_a)
    if last > 1:
        wave(1)
    n = gather_in(2)
    spread_out(3, plain_total(2, n))
    if last > 2:
        wave(2)
    n = gather_in(3)
    s0, s1 = unpack(plain_total(3, n))
    bgrad[...] = s0
    ngrad[...] = s1
    m1 = group_sum(s0 * gain) / everything
    m2 = group_sum(s1 * gain) / everything

    def to_input(i, c):
        f, r = lax.div(i, rows), lax.rem(i, rows)
        at_row = pl.ds(pl.multiple_of(i * width, 16), width)
        xhat = (latent[f, r].astype(F32) - mean) * rstd
        gx = acc[at_row, :] * gain
        grad_latent[f, r] = (g32[at_row, :] + rstd * (gx - m1 - xhat * m2)).astype(BF16)
        return c

    lax.fori_loop(0, frames * rows, to_input, 0)
    for w in range(3, last):
        wave(w)

    for u in range(UA):
        YB[y, u] = DA[core, u, x, z]
    for u in range(UB):
        YB[y, UA + u] = DB[core, u, z, x]

    def y_copy(k):
        yy = lax.rem(y + k, ny)
        return remote(YB.at[y], YB.at[y], y_s.at[k], y_r.at[k], at(yy, x, core), z)

    for k in range(1, ny):
        y_copy(k).start()
    for k in range(1, ny):
        y_copy(k).wait()
    total = YB[0]
    for k in range(1, ny):
        total = total + YB[k]
    XG[x, core] = total

    def to_x(src, units, up, i):
        first, many = units
        ref = XG.at[src, core, pl.ds(first, many)]
        return remote(ref, ref, xg_s.at[i], xg_r.at[i], at(y, up_x if up else dn_x, core), z)

    def to_core(src, i):
        ref = XG.at[src, core]
        return remote(ref, ref, cg_s.at[i], cg_r.at[i], at(y, x, other), z)

    whole = (0, UA + UB)
    step1 = [to_x(x, whole, True, 0), to_x(x, whole, False, 1)]
    cores = [to_core(x, 0), to_core(dn_x, 1), to_core(up_x, 2), to_core(lax.rem(x + 2, nx), 3)]
    for c in step1 + cores[:1]:
        c.start()
    step1[0].wait_recv()
    step2 = [to_x(dn_x, (0, UA), True, 2), to_x(up_x, (UA, UB), False, 3)]
    step2[0].start()
    cores[1].start()
    step1[1].wait_recv()
    step2[1].start()
    cores[2].start()
    for c in step2:
        c.wait_recv()
    cores[3].start()
    for c in cores:
        c.wait_recv()
    for xx in range(nx):
        for cc in range(2):
            rows_ = slice(xx * per, (xx + 1) * per)
            wgrad[:, :, rows_, cc * half : (cc + 1) * half] = XG[xx, cc]

    for c in step1 + step2 + cores:
        c.wait_send()

    def drain_a(u, c):
        to_sibling_a(u).wait_send()
        for ring, s in plan_a:
            ring.sent(u, s)
        return c

    def drain_b(u, c):
        to_sibling_b(u).wait_send()
        for ring, s in plan_b:
            ring.sent(u, s)
        return c

    lax.fori_loop(0, UA, drain_a, 0)
    lax.fori_loop(0, UB, drain_b, 0)


def per_device(nx, ny, nz, latent, target, conv_weight, gain, bias):
    frames, rows, width, ch = latent.shape
    size = frames * rows * width
    per, half = ch // (nx * nz), ch // 2
    sx, sz = nx // 2, nz // 2
    units = UA + UB
    tile = (3, per, half)
    V, D = pltpu.VMEM, pltpu.SemaphoreType.DMA
    big = (2 * frames, rows + 2, width, 3 * ch)
    scratch = [
        V((2 * frames, rows + 2, width, ch), BF16),
        V(big, BF16),
        V(big, BF16),
        V((2 * frames, rows + 2, width, ch), BF16),
        V((size, ch), F32),
        V((size, ch), F32),
        V((9, 3 * ch, ch), BF16),
        V((9, 3 * ch, ch), BF16),
        V((frames, rows, width, ch), BF16),
        V((ch, size), F32),
        V((ch, size), F32),
        V((2, UA, nx, nz) + tile, F32),
        V((2, UB, nz, nx) + tile, F32),
        V((UA, nx, nz) + tile, F32),
        V((UB, nz, nx) + tile, F32),
        V((UA, nz // 2) + tile, F32),
        V((UA, nz - nz // 2) + tile, F32),
        V((UA, max(sx - 1, 1), 2, nz) + tile, F32),
        V((UA, 2, per, half), F32),
        V((UA, 1, per, half), F32),
        V((UA, max(sz - 1, 1), 2) + tile, F32),
        V((UB, nx // 2) + tile, F32),
        V((UB, nx - nx // 2) + tile, F32),
        V((UB, max(sz - 1, 1), 2, nx) + tile, F32),
        V((UB, 2, per, half), F32),
        V((UB, 1, per, half), F32),
        V((UB, max(sx - 1, 1), 2) + tile, F32),
        V((ny, units) + tile, F32),
        V((nx, 2, units) + tile, F32),
        V((4, max(2 * nz, nx * ny), 8, half), F32),
        D((2,)),
        D((5,)), D((5,)), D((5,)), D((5,)),
        D((4, max(2 * nz, nx * ny))), D((4, max(2 * nz, nx * ny))),
        D((units,)), D((units,)),
        D((units, sx + sz, 2)), D((units, sx + sz, 2)),
        D((ny,)), D((ny,)),
        D((4,)), D((4,)), D((4,)), D((4,)),
    ]
    vm = pl.BlockSpec(memory_space=pltpu.VMEM)
    anywhere = pl.BlockSpec(memory_space=pl.ANY)
    outs = [
        jax.ShapeDtypeStruct(latent.shape, BF16),
        jax.ShapeDtypeStruct(latent.shape, BF16),
        jax.ShapeDtypeStruct((9, 3, ch // nz, ch), F32),
        jax.ShapeDtypeStruct((1, ch), F32),
        jax.ShapeDtypeStruct((1, ch), F32),
    ]
    decoded, grad_latent, wgrad, ngrad, bgrad = pl.pallas_call(
        functools.partial(kernel, nx, ny, nz, size),
        out_shape=outs,
        in_specs=[vm, anywhere, anywhere, vm, vm],
        out_specs=[vm] * 5,
        scratch_shapes=scratch,
        compiler_params=pltpu.CompilerParams(
            collective_id=0, has_side_effects=True, vmem_limit_bytes=60 * 2**20
        ),
        name="block",
    )(
        latent,
        target,
        conv_weight.reshape(9, 3 * ch, ch),
        gain.reshape(1, ch),
        bias.reshape(1, ch),
    )
    wgrad = jnp.swapaxes(wgrad.reshape(3, 3, 3, ch // nz, ch), 3, 4)
    return decoded, grad_latent, wgrad, ngrad.reshape(ch), bgrad.reshape(ch)


def solution(mesh, nx=4):
    nt, nz = mesh.shape["tm"], mesh.shape["height"]
    ny = nt // (2 * nx)
    in_specs = (P("tm", "height", None, None), P("tm", "height", None, None), P(), P(), P())
    out_specs = (
        P("tm", "height", None, None),
        P("tm", "height", None, None),
        P(None, None, None, None, "height"),
        P(),
        P(),
    )
    return jax.shard_map(
        functools.partial(per_device, nx, ny, nz),
        mesh=mesh,
        in_specs=in_specs,
        out_specs=out_specs,
        check_vma=False,
    )
```

```python
import functools

import jax
import jax.numpy as jnp
from jax import lax
from jax.experimental import pallas as pl
from jax.experimental.pallas import tpu as pltpu
from jax.sharding import PartitionSpec as P

NORM_GROUPS = 32
EPS = 1e-06
MESH = pl.DeviceIdType.MESH
F32 = jnp.float32
BF16 = jnp.bfloat16
TAPS = 9


def group_sum(v):
    lane = lax.broadcasted_iota(jnp.int32, v.shape, 1)
    width = v.shape[1]
    for k in (1, 2, 4):
        other = jnp.where(
            lax.rem(lax.div(lane, k), 2) == 1,
            pltpu.roll(v, k, 1),
            pltpu.roll(v, width - k, 1),
        )
        v = v + other
    return v


def pack(a, b):
    half = a.shape[1] // 2
    return jnp.concatenate(
        [a[:, :half], a[:, half:], b[:, :half], b[:, half:], jnp.zeros((4, half), F32)], axis=0
    )


def unpack(v):
    a = jnp.concatenate([v[0:1], v[1:2]], axis=1)
    b = jnp.concatenate([v[2:3], v[3:4]], axis=1)
    return a, b


def kernel(
    nx, ny, nz, shape,
    latent_hbm, target_hbm, w_hbm, gain_hbm, bias_hbm,
    decoded_hbm, grad_latent_hbm, wgrad_hbm, ngrad_hbm, bgrad_hbm,
    L, A, G, graw, g32, acc, W, WT, target, gain_ref, bias_ref,
    decoded, grad_latent, wgrad, ngrad, bgrad,
    gta, gtb, DP, DZ, CP, CZ,
    PH, PF, ZH, ZF, Q2, Q, Q3, ZX, XG, AR,
    in_sem, out_sem, lat_s, lat_r, gh_s, gh_r, ar_s, ar_r, co_s, co_r,
    p_s, p_r, z_s, z_r, q_s, q_r, q3_s, q3_r, zx_s, zx_r, xg_s, xg_r, cg_s, cg_r,
):
    t = lax.axis_index("tm")
    z = lax.axis_index("height")
    nt = 2 * nx * ny
    core = lax.rem(t, 2)
    x = lax.rem(lax.div(t, 2), nx)
    y = lax.div(t, 2 * nx)
    frames, rows, width, ch = shape
    other = 1 - core

    def at(yy, xx, cc):
        return (yy * nx + xx) * 2 + cc

    def remote(src, dst, ss, rs, tt, zz):
        return pltpu.make_async_remote_copy(
            src_ref=src, dst_ref=dst, send_sem=ss, recv_sem=rs,
            device_id=(tt, zz), device_id_type=MESH,
        )

    def loop(lo, hi, f):
        def step(i, c):
            f(i)
            return c

        lax.fori_loop(lo, hi, step, 0)

    up_t, dn_t = lax.rem(t + 1, nt), lax.rem(t + nt - 1, nt)
    up_z, dn_z = lax.rem(z + 1, nz), lax.rem(z + nz - 1, nz)

    latent = L.at[pl.ds(frames, frames), pl.ds(1, rows)]
    latent_in = pltpu.make_async_copy(latent_hbm, latent, in_sem.at[0])
    latent_in.start()

    n1, n2 = 2 * nz, nx * ny
    me1, me2 = core * nz + z, y * nx + x

    def peer1(k):
        p = lax.rem(me1 + k, n1)
        return at(y, x, lax.div(p, nz)), lax.rem(p, nz)

    def peer2(k):
        p = lax.rem(me2 + k, n2)
        return p * 2 + core, z

    barrier = pltpu.get_barrier_semaphore()

    def greet(tt, zz):
        pl.semaphore_signal(barrier, inc=1, device_id=(tt, zz), device_id_type=MESH)

    loop(1, n1, lambda k: greet(*peer1(k)))
    loop(1, n2, lambda k: greet(*peer2(k)))
    for tt in (up_t, dn_t):
        for zz in (dn_z, z, up_z):
            greet(tt, zz)

    gain_in = pltpu.make_async_copy(gain_hbm, gain_ref, in_sem.at[1])
    bias_in = pltpu.make_async_copy(bias_hbm, bias_ref, in_sem.at[2])
    weights_in = pltpu.make_async_copy(w_hbm, W, in_sem.at[3])
    target_in = pltpu.make_async_copy(target_hbm, target, in_sem.at[4])
    for c in (gain_in, bias_in, weights_in, target_in):
        c.start()
    latent_in.wait()

    def eights(v):
        return jnp.sum(v.reshape(width // 8, 8, ch), axis=0)

    def sum_rows(i, total):
        return total + eights(latent[lax.div(i, rows), lax.rem(i, rows)].astype(F32))

    count = frames * rows * width * 8
    total = lax.fori_loop(0, frames * rows, sum_rows, jnp.zeros((8, ch), F32))
    mean_l = group_sum(jnp.sum(total, axis=0, keepdims=True)) / count

    def sum_squares(i, total):
        v = latent[lax.div(i, rows), lax.rem(i, rows)].astype(F32) - mean_l
        return total + eights(v * v)

    total = lax.fori_loop(0, frames * rows, sum_squares, jnp.zeros((8, ch), F32))
    sq_l = group_sum(jnp.sum(total, axis=0, keepdims=True))

    pl.semaphore_wait(barrier, (n1 - 1) + (n2 - 1) + 6)

    def exchange(stage, k):
        me, peer = (me1, peer1) if stage % 2 == 0 else (me2, peer2)
        slot = AR.at[stage, me]
        return remote(slot, slot, ar_s.at[stage, k], ar_r.at[stage, k], *peer(k))

    def spread_out(stage, value):
        me, n = (me1, n1) if stage % 2 == 0 else (me2, n2)
        AR[stage, me] = value
        loop(1, n, lambda k: exchange(stage, k).start())

    def gather_in(stage):
        n = n1 if stage % 2 == 0 else n2
        loop(1, n, lambda k: exchange(stage, k).wait())
        return n

    def plain_total(stage, n):
        total = AR[stage, 0]
        for k in range(1, n):
            total = total + AR[stage, k]
        return total

    def moments(stage, n, members):
        mean = plain_total(stage, n)[0:2] / n
        sq = jnp.zeros_like(mean)
        for k in range(n):
            d = AR[stage, k, 0:2] - mean
            sq = sq + (AR[stage, k, 2:4] + (d * d) * members)
        return jnp.concatenate([mean, sq, jnp.zeros((4, mean.shape[1]), F32)], axis=0)

    spread_out(0, pack(mean_l, sq_l))

    def halo(block, buf, first, away, tt, ss, rs):
        edge0, edge1 = block.at[:, 0], block.at[:, rows - 1]
        mine, theirs = pl.ds(first, frames), pl.ds(away, frames)
        return [
            remote(block, buf.at[theirs, pl.ds(1, rows)], ss.at[0], rs.at[0], tt, z),
            remote(edge1, buf.at[mine, 0], ss.at[1], rs.at[1], t, up_z),
            remote(edge0, buf.at[mine, rows + 1], ss.at[2], rs.at[2], t, dn_z),
            remote(edge1, buf.at[theirs, 0], ss.at[3], rs.at[3], tt, up_z),
            remote(edge0, buf.at[theirs, rows + 1], ss.at[4], rs.at[4], tt, dn_z),
        ]

    lat_halo = halo(latent, L, frames, 0, up_t, lat_s, lat_r)
    for c in lat_halo:
        c.start()

    def flip(u):
        for kc in range(3):
            WT[8 - u, (2 - kc) * ch : (3 - kc) * ch, :] = W[u, kc * ch : (kc + 1) * ch, :].T

    n = gather_in(0)
    spread_out(1, moments(0, n, count))
    weights_in.wait()
    loop(0, TAPS, flip)
    gain_in.wait()
    bias_in.wait()
    n = gather_in(1)
    mean, sq = unpack(moments(1, n, count * n1))
    everything = count * n1 * n2
    rstd = lax.rsqrt(sq / everything + EPS)
    gain, bias = gain_ref[...], bias_ref[...]
    scale = rstd * gain

    for c in lat_halo:
        c.wait()

    col = lax.broadcasted_iota(jnp.int32, (width, ch), 0)

    def store_shifts(buf, f, r, v):
        buf[f, r, :, 0:ch] = jnp.where(col == 0, 0.0, pltpu.roll(v, 1, 0)).astype(BF16)
        buf[f, r, :, ch : 2 * ch] = v.astype(BF16)
        buf[f, r, :, 2 * ch : 3 * ch] = jnp.where(
            col == width - 1, 0.0, pltpu.roll(v, width - 1, 0)
        ).astype(BF16)

    def inside(f, r, lone, edge):
        top = jnp.logical_or(r > 0, z > 0)
        low = jnp.logical_or(r < rows + 1, z < nz - 1)
        return jnp.logical_and(jnp.logical_or(lone, edge), jnp.logical_and(top, low))

    def activate(i):
        f, r = lax.div(i, rows + 2), lax.rem(i, rows + 2)
        zz = (L[f, r].astype(F32) - mean) * scale + bias
        v = zz / (1.0 + jnp.exp(-zz))
        keep = inside(f, r, f >= frames, t > 0)
        store_shifts(A, f, r, jnp.where(keep, v, 0.0))

    loop(0, 2 * frames * (rows + 2), activate)

    size = frames * rows * width

    def piece(buf, u):
        kt, kr = lax.div(u, 3), lax.rem(u, 3)
        return buf[pl.ds(kt, frames), pl.ds(kr, rows)].reshape(size, 3 * ch)

    def conv(buf, w):
        acc[...] = jnp.dot(piece(buf, 0), w[0], preferred_element_type=F32)

        def tap(u):
            acc[...] += jnp.dot(piece(buf, u), w[u], preferred_element_type=F32)

        loop(1, TAPS, tap)

    conv(A, W)
    target_in.wait()

    def finish(i):
        f, r = lax.div(i, rows), lax.rem(i, rows)
        at_row = pl.ds(pl.multiple_of(i * width, 16), width)
        out = latent[f, r].astype(F32) + acc[at_row, :]
        decoded[f, r] = out.astype(BF16)
        g = out - target[f, r].astype(F32)
        g32[at_row, :] = g
        graw[f, 1 + r] = g.astype(BF16)

    loop(0, frames * rows, finish)

    own = graw.at[pl.ds(0, frames), pl.ds(1, rows)]
    g_halo = halo(own, graw, 0, frames, dn_t, gh_s, gh_r)
    for c in g_halo:
        c.start()
    decoded_out = pltpu.make_async_copy(decoded, decoded_hbm, out_sem.at[0])
    decoded_out.start()

    per = ch // (nx * nz)
    half = ch // 2
    for b in range(ch // 128):
        for q in range(size // 128):
            cols = slice(q * 128, (q + 1) * 128)
            block = g32[cols, b * 128 : (b + 1) * 128].T
            gtb[b * 128 : (b + 1) * 128, cols] = block
            for i in range(128 // per):
                zz, cc = divmod(b * (128 // per) + i, nx)
                gta[(cc * nz + zz) * per : (cc * nz + zz + 1) * per, cols] = (
                    block[i * per : (i + 1) * per]
                )

    def core_p(u):
        return remote(DP.at[other, u], CP.at[u], co_s.at[u], co_r.at[u], at(y, x, other), z)

    def core_z():
        return remote(DZ.at[other], CZ, co_s.at[8], co_r.at[8], at(y, x, other), z)

    def kernel_term(gt, unit, store):
        res = jnp.dot(gt[...].astype(BF16), piece(A, unit), preferred_element_type=F32)
        for kc in range(3):
            for h in range(2):
                lo = kc * ch + h * half
                store(h, kc, res[:, lo : lo + half])

    def term_p(u):
        def store(h, kc, v):
            DP[h, u, :, :, kc] = v.reshape(nx, nz, per, half)

        kernel_term(gta, u, store)
        core_p(u).start()

    def term_z():
        def store(h, kc, v):
            DZ[h, :, :, kc] = v.reshape(nz, nx, per, half)

        kernel_term(gtb, 8, store)
        core_z().start()

    def along(u, d):
        s = lax.div(u, 4)
        xx = lax.rem(x + (1 - s) * d + nx, nx)
        yy = lax.rem(y + s * d + ny, ny)
        return x * (1 - s) + y * s, at(yy, xx, core)

    def ring_p(u, step):
        me, up = along(u, 1)
        _, down = along(u, -1)
        sems = [(p_s.at[u, step, d], p_r.at[u, step, d]) for d in range(2)]
        if step == 0:
            far = DP.at[core, u, lax.rem(me + 2, 4)]
            return [
                remote(far.at[pl.ds(0, nz // 2)], PH.at[u, 0], *sems[0], up, z),
                remote(far.at[pl.ds(nz // 2, nz // 2)], PH.at[u, 1], *sems[1], down, z),
            ]
        return [
            remote(DP.at[core, u, lax.rem(me + 1, 4)], PF.at[u, 0], *sems[0], up, z),
            remote(DP.at[core, u, lax.rem(me + 3, 4)], PF.at[u, 1], *sems[1], down, z),
        ]

    def recv_p(u, step):
        me, _ = along(u, 1)
        for c in ring_p(u, step):
            c.wait_recv()
        if step == 0:
            right, left = lax.rem(me + 1, 4), lax.rem(me + 3, 4)
            h = nz // 2
            DP[core, u, right, 0:h] = DP[core, u, right, 0:h] + PH[u, 0]
            DP[core, u, left, h:nz] = DP[core, u, left, h:nz] + PH[u, 1]
        else:
            DP[core, u, me] = DP[core, u, me] + PF[u, 0] + PF[u, 1]

    def order(i):
        return lax.rem(i, 2) * 4 + lax.div(i, 2)

    def first_p(u):
        core_p(u).wait_recv()
        DP[core, u] = DP[core, u] + CP[u]
        for c in ring_p(u, 0):
            c.start()

    sz = nz // 2

    def ring_z(step):
        sems = [(z_s.at[step, d], z_r.at[step, d]) for d in range(2)]
        if step == 0:
            far = DZ.at[core, lax.rem(z + sz, nz)]
            return [
                remote(far.at[pl.ds(0, nx // 2)], ZH.at[0], *sems[0], t, up_z),
                remote(far.at[pl.ds(nx // 2, nx // 2)], ZH.at[1], *sems[1], t, dn_z),
            ]
        up, down = lax.rem(z + sz - step, nz), lax.rem(z + nz - sz + step, nz)
        return [
            remote(DZ.at[core, up], ZF.at[step - 1, 0], *sems[0], t, up_z),
            remote(DZ.at[core, down], ZF.at[step - 1, 1], *sems[1], t, dn_z),
        ]

    def recv_z(step):
        for c in ring_z(step):
            c.wait_recv()
        left = lax.rem(z + nz - 1 + sz - step, nz)
        right = lax.rem(z + nz + 1 - sz + step, nz)
        if step == 0:
            h = nx // 2
            DZ[core, left, 0:h] = DZ[core, left, 0:h] + ZH[0]
            DZ[core, right, h:nx] = DZ[core, right, h:nx] + ZH[1]
        else:
            DZ[core, left] = DZ[core, left] + ZF[step - 1, 0]
            DZ[core, right] = DZ[core, right] + ZF[step - 1, 1]
        if step + 1 < sz:
            for c in ring_z(step + 1):
                c.start()

    term_p(order(0))

    def term_and_first(i):
        term_p(order(i))
        first_p(order(i - 1))

    loop(1, 8, term_and_first)
    term_z()
    first_p(7)
    core_z().wait_recv()
    DZ[core] = DZ[core] + CZ[...]
    for c in ring_z(0):
        c.start()

    def wave_0(i):
        u = order(i)
        recv_p(u, 0)
        for c in ring_p(u, 1):
            c.start()

    def cross(s, k):
        yy = lax.rem(y + (1 - s) * k, ny)
        xx = lax.rem(x + s * k, nx)
        me = x * (1 - s) + y * s
        u = 4 * s + yy * (1 - s) + xx * s
        return remote(
            DP.at[core, u, me], Q2.at[s, k], q_s.at[s, k], q_r.at[s, k], at(yy, xx, core), z
        )

    def wave_1(i):
        u = order(i)
        recv_p(u, 1)
        s, v = lax.div(u, 4), lax.rem(u, 4)
        here = y * (1 - s) + x * s

        @pl.when(v != here)
        def _():
            cross(s, lax.rem(v - here + 4, 4)).start()

    def sum_z(k):
        c = lax.rem(z + k, nz)
        return remote(Q.at[c], Q3.at[k], q3_s.at[k], q3_r.at[k], t, c)

    def wave_2():
        for s in range(2):
            loop(1, 4, lambda k: cross(s, k).wait_recv())
            me, here = (x, y) if s == 0 else (y, x)
            Q[:, s] = DP[core, 4 * s + here, me] + Q2[s, 1] + Q2[s, 2] + Q2[s, 3]
        loop(1, nz, lambda k: sum_z(k).start())

    def z_to_x(k):
        xx = lax.rem(x + k, nx)
        return remote(
            DZ.at[core, z, xx], ZX.at[k], zx_s.at[k], zx_r.at[k], at(y, xx, core), z
        )

    me_xy = y * nx + x

    def publish(k):
        p = lax.rem(me_xy + k, n2)
        slot = XG.at[me_xy, core]
        return remote(slot, slot, xg_s.at[k], xg_r.at[k], p * 2 + core, z)

    def to_core(k):
        slot = XG.at[lax.rem(me_xy + n2 - k, n2), core]
        return remote(slot, slot, cg_s.at[k], cg_r.at[k], at(y, x, other), z)

    def wave_3():
        loop(1, nx, lambda k: z_to_x(k).wait_recv())
        total = DZ[core, z, x]
        for k in range(1, nx):
            total = total + ZX[k]
        XG[me_xy, core, 2] = total
        loop(1, nz, lambda k: sum_z(k).wait_recv())
        total = Q[z]
        for k in range(1, nz):
            total = total + Q3[k]
        XG[me_xy, core, 0:2] = total
        loop(1, n2, lambda k: publish(k).start())
        to_core(0).start()

    loop(0, 8, wave_0)
    recv_z(0)

    for c in g_halo:
        c.wait()

    def shift_gradient(i):
        f, r = lax.div(i, rows + 2), lax.rem(i, rows + 2)
        keep = inside(f, r, f < frames, t < nt - 1)
        store_shifts(G, f, r, jnp.where(keep, graw[f, r].astype(F32), 0.0))

    loop(0, 2 * frames * (rows + 2), shift_gradient)
    for step in range(1, min(2, sz)):
        recv_z(step)
    conv(G, WT)
    for step in range(2, min(3, sz)):
        recv_z(step)

    def through_norm(i, carry):
        s0, s1 = carry
        f, r = lax.div(i, rows), lax.rem(i, rows)
        at_row = pl.ds(pl.multiple_of(i * width, 16), width)
        d = latent[f, r].astype(F32) - mean
        zz = d * scale + bias
        sig = 1.0 / (1.0 + jnp.exp(-zz))
        gz = acc[at_row, :] * sig * (1.0 + zz * (1.0 - sig))
        acc[at_row, :] = gz
        return s0 + eights(gz), s1 + eights(gz * (d * rstd))

    zero = jnp.zeros((8, ch), F32)
    s0, s1 = lax.fori_loop(0, frames * rows, through_norm, (zero, zero))
    spread_out(2, pack(jnp.sum(s0, axis=0, keepdims=True), jnp.sum(s1, axis=0, keepdims=True)))
    for step in range(3, sz):
        recv_z(step)
    loop(1, nx, lambda k: z_to_x(k).start())
    loop(0, 8, wave_1)
    n = gather_in(2)
    spread_out(3, plain_total(2, n))
    wave_2()
    n = gather_in(3)
    s0, s1 = unpack(plain_total(3, n))
    bgrad[...] = s0
    ngrad[...] = s1
    m1 = group_sum(s0 * gain) / everything
    m2 = group_sum(s1 * gain) / everything

    def to_input(i):
        f, r = lax.div(i, rows), lax.rem(i, rows)
        at_row = pl.ds(pl.multiple_of(i * width, 16), width)
        xhat = (latent[f, r].astype(F32) - mean) * rstd
        gx = acc[at_row, :] * gain
        grad_latent[f, r] = (g32[at_row, :] + rstd * (gx - m1 - xhat * m2)).astype(BF16)

    loop(0, frames * rows, to_input)
    outs = [
        decoded_out,
        pltpu.make_async_copy(grad_latent, grad_latent_hbm, out_sem.at[1]),
        pltpu.make_async_copy(ngrad, ngrad_hbm, out_sem.at[2]),
        pltpu.make_async_copy(bgrad, bgrad_hbm, out_sem.at[3]),
        pltpu.make_async_copy(wgrad, wgrad_hbm, out_sem.at[4]),
    ]
    for c in outs[1:4]:
        c.start()

    wave_3()

    def pass_on(k):
        publish(k).wait_recv()
        to_core(k).start()

    loop(1, n2, pass_on)
    loop(0, n2, lambda k: to_core(k).wait_recv())
    for cc in range(2):
        lanes = slice(cc * half, (cc + 1) * half)
        for xx in range(nx):
            for yy in range(ny):
                p = yy * nx + xx
                wgrad[yy, :, xx * per : (xx + 1) * per, lanes] = XG[p, cc, 0]
                wgrad[4 + xx, :, yy * per : (yy + 1) * per, lanes] = XG[p, cc, 1]
            total = XG[xx, cc, 2]
            for yy in range(1, ny):
                total = total + XG[yy * nx + xx, cc, 2]
            wgrad[8, :, xx * per : (xx + 1) * per, lanes] = total
    outs[4].start()

    def drain(u):
        core_p(u).wait_send()
        for step in range(2):
            for c in ring_p(u, step):
                c.wait_send()

    loop(0, 8, drain)
    core_z().wait_send()
    for step in range(sz):
        for c in ring_z(step):
            c.wait_send()

    def drain_cross(k):
        cross(0, k).wait_send()
        cross(1, k).wait_send()
        z_to_x(k).wait_send()

    loop(1, 4, drain_cross)
    loop(1, nz, lambda k: sum_z(k).wait_send())
    loop(1, n2, lambda k: publish(k).wait_send())
    loop(0, n2, lambda k: to_core(k).wait_send())
    for c in outs:
        c.wait()


def hand_over(*refs):
    n = len(refs) // 3
    given, out, held, sem = refs[:n], refs[n : 2 * n], refs[2 * n : 3 * n], refs[-1]
    into = [pltpu.make_async_copy(given[i], held[i], sem.at[0, i]) for i in range(n)]
    onto = [pltpu.make_async_copy(held[i], out[i], sem.at[1, i]) for i in range(n)]
    for c in into:
        c.start()
    for a, b in zip(into, onto):
        a.wait()
        b.start()
    for c in onto:
        c.wait()


def per_device(nx, ny, nz, latent, target, conv_weight, gain, bias):
    frames, rows, width, ch = latent.shape
    size = frames * rows * width
    per, half = ch // (nx * nz), ch // 2
    sz, n2 = nz // 2, nx * ny
    tile = (3, per, half)
    V, D = pltpu.VMEM, pltpu.SemaphoreType.DMA
    padded = (2 * frames, rows + 2, width)
    block = (frames, rows, width, ch)
    most = max(2 * nz, n2)
    scratch = [
        V(padded + (ch,), BF16),
        V(padded + (3 * ch,), BF16),
        V(padded + (3 * ch,), BF16),
        V(padded + (ch,), BF16),
        V((size, ch), F32),
        V((size, ch), F32),
        V((TAPS, 3 * ch, ch), BF16),
        V((TAPS, 3 * ch, ch), BF16),
        V(block, BF16),
        V((1, ch), F32),
        V((1, ch), F32),
        V(block, BF16),
        V(block, BF16),
        V((TAPS, 3, ch // nz, ch), F32),
        V((1, ch), F32),
        V((1, ch), F32),
        V((ch, size), F32),
        V((ch, size), F32),
        V((2, 8, nx, nz) + tile, F32),
        V((2, nz, nx) + tile, F32),
        V((8, nx, nz) + tile, F32),
        V((nz, nx) + tile, F32),
        V((8, 2, nz // 2) + tile, F32),
        V((8, 2, nz) + tile, F32),
        V((2, nx // 2) + tile, F32),
        V((max(sz - 1, 1), 2, nx) + tile, F32),
        V((2, 4, nz) + tile, F32),
        V((nz, 2) + tile, F32),
        V((nz, 2) + tile, F32),
        V((nx,) + tile, F32),
        V((n2, 2, 3) + tile, F32),
        V((4, most, 8, half), F32),
        D((5,)), D((5,)),
        D((5,)), D((5,)), D((5,)), D((5,)),
        D((4, most)), D((4, most)),
        D((9,)), D((9,)),
        D((8, 2, 2)), D((8, 2, 2)),
        D((sz, 2)), D((sz, 2)),
        D((2, 4)), D((2, 4)),
        D((nz,)), D((nz,)),
        D((nx,)), D((nx,)),
        D((n2,)), D((n2,)), D((n2,)), D((n2,)),
    ]
    anywhere = pl.BlockSpec(memory_space=pl.ANY)
    shapes = [
        jax.ShapeDtypeStruct(latent.shape, BF16),
        jax.ShapeDtypeStruct(latent.shape, BF16),
        jax.ShapeDtypeStruct((TAPS, 3, ch // nz, ch), F32),
        jax.ShapeDtypeStruct((1, ch), F32),
        jax.ShapeDtypeStruct((1, ch), F32),
    ]
    results = pl.pallas_call(
        functools.partial(kernel, nx, ny, nz, latent.shape),
        out_shape=shapes,
        in_specs=[anywhere] * 5,
        out_specs=[anywhere] * 5,
        scratch_shapes=scratch,
        compiler_params=pltpu.CompilerParams(
            collective_id=0, has_side_effects=True, vmem_limit_bytes=60 * 2**20
        ),
        name="block",
    )(
        latent,
        target,
        conv_weight.reshape(TAPS, 3 * ch, ch),
        gain.reshape(1, ch),
        bias.reshape(1, ch),
    )
    decoded, grad_latent, wgrad, ngrad, bgrad = pl.pallas_call(
        hand_over,
        out_shape=shapes,
        in_specs=[anywhere] * 5,
        out_specs=[anywhere] * 5,
        scratch_shapes=[V(o.shape, o.dtype) for o in shapes] + [D((2, 5))],
        name="hand_over",
    )(*results)
    wgrad = jnp.swapaxes(wgrad.reshape(3, 3, 3, ch // nz, ch), 3, 4)
    return decoded, grad_latent, wgrad, ngrad.reshape(ch), bgrad.reshape(ch)


def solution(mesh, nx=4):
    nt, nz = mesh.shape["tm"], mesh.shape["height"]
    ny = nt // (2 * nx)
    in_specs = (P("tm", "height", None, None), P("tm", "height", None, None), P(), P(), P())
    out_specs = (
        P("tm", "height", None, None),
        P("tm", "height", None, None),
        P(None, None, None, None, "height"),
        P(),
        P(),
    )
    return jax.shard_map(
        functools.partial(per_device, nx, ny, nz),
        mesh=mesh,
        in_specs=in_specs,
        out_specs=out_specs,
        check_vma=False,
    )
```

```python
import functools

import jax
import jax.numpy as jnp
from jax import lax
from jax.experimental import pallas as pl
from jax.experimental.pallas import tpu as pltpu
from jax.sharding import PartitionSpec as P

NORM_GROUPS = 32
EPS = 1e-06
MESH = pl.DeviceIdType.MESH
F32 = jnp.float32
BF16 = jnp.bfloat16
TAPS = 9


def group_sum(v):
    lane = lax.broadcasted_iota(jnp.int32, v.shape, 1)
    width = v.shape[1]
    for k in (1, 2, 4):
        other = jnp.where(
            (lane & k) != 0,
            pltpu.roll(v, k, 1),
            pltpu.roll(v, width - k, 1),
        )
        v = v + other
    return v


def pack(a, b):
    half = a.shape[1] // 2
    return jnp.concatenate(
        [a[:, :half], a[:, half:], b[:, :half], b[:, half:], jnp.zeros((4, half), F32)], axis=0
    )


def unpack(v):
    a = jnp.concatenate([v[0:1], v[1:2]], axis=1)
    b = jnp.concatenate([v[2:3], v[3:4]], axis=1)
    return a, b


FAR_FIRST = (
    (4, 12, 3, 5, 11, 13, 2, 6, 10, 14, 1, 7, 9, 15, 8),
    (10, 6, 14, 9, 11, 2, 8, 5, 7, 13, 15, 3, 1, 4, 12),
)


def kernel(
    nx, ny, nz, shape,
    latent_hbm, target_hbm, w_hbm, gain_hbm, bias_hbm,
    decoded_hbm, grad_latent_hbm, wgrad_hbm, ngrad_hbm, bgrad_hbm,
    L, A, G, graw, g32, acc, W, WT, target, gain_ref, bias_ref,
    decoded, grad_latent, wgrad, ngrad, bgrad,
    gta, gtb, gta16, gtb16, DP, DZ, CP, CZ,
    PH, PF, ZH, ZF, Q2, Q, Q3, ZX, XG, XZ, AR,
    in_sem, out_sem, lat_s, lat_r, gh_s, gh_r, ar_s, ar_r, co_s, co_r,
    p_s, p_r, z_s, z_r, q_s, q_r, q3_s, q3_r, zx_s, zx_r, xg_s, xg_r, cg_s, cg_r,
    xz_s, xz_r, cz_s, cz_r,
):
    t = lax.axis_index("tm")
    z = lax.axis_index("height")
    nt = 2 * nx * ny
    core = lax.rem(t, 2)
    x = lax.rem(lax.div(t, 2), nx)
    y = lax.div(t, 2 * nx)
    frames, rows, width, ch = shape
    other = 1 - core

    def at(yy, xx, cc):
        return (yy * nx + xx) * 2 + cc

    def remote(src, dst, ss, rs, tt, zz):
        return pltpu.make_async_remote_copy(
            src_ref=src, dst_ref=dst, send_sem=ss, recv_sem=rs,
            device_id=(tt, zz), device_id_type=MESH,
        )

    def loop(lo, hi, f):
        def step(i, c):
            f(i)
            return c

        lax.fori_loop(lo, hi, step, 0)

    up_t, dn_t = lax.rem(t + 1, nt), lax.rem(t + nt - 1, nt)
    up_z, dn_z = lax.rem(z + 1, nz), lax.rem(z + nz - 1, nz)

    latent = L.at[pl.ds(frames, frames), pl.ds(1, rows)]
    latent_in = pltpu.make_async_copy(latent_hbm, latent, in_sem.at[0])
    latent_in.start()

    n1, n2 = 2 * nz, nx * ny
    me1, me2 = core * nz + z, y * nx + x

    def peer1(k):
        p = lax.rem(me1 + k, n1)
        return at(y, x, lax.div(p, nz)), lax.rem(p, nz)

    def peer2(k):
        p = lax.rem(me2 + k, n2)
        return p * 2 + core, z

    barrier = pltpu.get_barrier_semaphore()

    def greet(tt, zz):
        pl.semaphore_signal(barrier, inc=1, device_id=(tt, zz), device_id_type=MESH)

    loop(1, n1, lambda k: greet(*peer1(k)))
    loop(1, n2, lambda k: greet(*peer2(k)))
    for tt in (up_t, dn_t):
        for zz in (dn_z, z, up_z):
            greet(tt, zz)

    gain_in = pltpu.make_async_copy(gain_hbm, gain_ref, in_sem.at[1])
    bias_in = pltpu.make_async_copy(bias_hbm, bias_ref, in_sem.at[2])
    weights_in = pltpu.make_async_copy(w_hbm, W, in_sem.at[3])
    target_in = pltpu.make_async_copy(target_hbm, target, in_sem.at[4])
    for c in (gain_in, bias_in, weights_in, target_in):
        c.start()
    latent_in.wait()

    def eights(v):
        return jnp.sum(v.reshape(width // 8, 8, ch), axis=0)

    def sum_rows(i, total):
        return total + eights(latent[lax.div(i, rows), lax.rem(i, rows)].astype(F32))

    count = frames * rows * width * 8
    total = lax.fori_loop(0, frames * rows, sum_rows, jnp.zeros((8, ch), F32))
    mean_l = group_sum(jnp.sum(total, axis=0, keepdims=True)) / count

    def sum_squares(i, total):
        v = latent[lax.div(i, rows), lax.rem(i, rows)].astype(F32) - mean_l
        return total + eights(v * v)

    total = lax.fori_loop(0, frames * rows, sum_squares, jnp.zeros((8, ch), F32))
    sq_l = group_sum(jnp.sum(total, axis=0, keepdims=True))

    pl.semaphore_wait(barrier, (n1 - 1) + (n2 - 1) + 6)

    def exchange(stage, k):
        me, peer = (me1, peer1) if stage % 2 == 0 else (me2, peer2)
        slot = AR.at[stage, me]
        return remote(slot, slot, ar_s.at[stage, k], ar_r.at[stage, k], *peer(k))

    def spread_out(stage, value):
        me, n = (me1, n1) if stage % 2 == 0 else (me2, n2)
        AR[stage, me] = value
        for k in FAR_FIRST[stage % 2]:
            if k < n:
                exchange(stage, k).start()

    def gather_in(stage):
        n = n1 if stage % 2 == 0 else n2
        loop(1, n, lambda k: exchange(stage, k).wait())
        return n

    def plain_total(stage, n):
        total = AR[stage, 0]
        for k in range(1, n):
            total = total + AR[stage, k]
        return total

    def moments(stage, n, members):
        mean = plain_total(stage, n)[0:2] / n
        sq = jnp.zeros_like(mean)
        for k in range(n):
            d = AR[stage, k, 0:2] - mean
            sq = sq + (AR[stage, k, 2:4] + (d * d) * members)
        return jnp.concatenate([mean, sq, jnp.zeros((4, mean.shape[1]), F32)], axis=0)

    spread_out(0, pack(mean_l, sq_l))

    def halo(block, buf, first, away, tt, ss, rs):
        edge0, edge1 = block.at[:, 0], block.at[:, rows - 1]
        mine, theirs = pl.ds(first, frames), pl.ds(away, frames)
        return [
            remote(block, buf.at[theirs, pl.ds(1, rows)], ss.at[0], rs.at[0], tt, z),
            remote(edge1, buf.at[mine, 0], ss.at[1], rs.at[1], t, up_z),
            remote(edge0, buf.at[mine, rows + 1], ss.at[2], rs.at[2], t, dn_z),
            remote(edge1, buf.at[theirs, 0], ss.at[3], rs.at[3], tt, up_z),
            remote(edge0, buf.at[theirs, rows + 1], ss.at[4], rs.at[4], tt, dn_z),
        ]

    lat_halo = halo(latent, L, frames, 0, up_t, lat_s, lat_r)
    for c in lat_halo:
        c.start()

    def flip(u):
        for kc in range(3):
            WT[8 - u, (2 - kc) * ch : (3 - kc) * ch, :] = W[u, kc * ch : (kc + 1) * ch, :].T

    n = gather_in(0)
    spread_out(1, moments(0, n, count))
    weights_in.wait()
    loop(0, TAPS, flip)
    gain_in.wait()
    bias_in.wait()
    n = gather_in(1)
    mean, sq = unpack(moments(1, n, count * n1))
    everything = count * n1 * n2
    rstd = lax.rsqrt(sq / everything + EPS)
    gain, bias = gain_ref[...], bias_ref[...]
    scale = rstd * gain

    for c in lat_halo:
        c.wait()

    col = lax.broadcasted_iota(jnp.int32, (width, ch), 0)

    def store_shifts(buf, f, r, v):
        buf[f, r, :, 0:ch] = jnp.where(col == 0, 0.0, pltpu.roll(v, 1, 0)).astype(BF16)
        buf[f, r, :, ch : 2 * ch] = v.astype(BF16)
        buf[f, r, :, 2 * ch : 3 * ch] = jnp.where(
            col == width - 1, 0.0, pltpu.roll(v, width - 1, 0)
        ).astype(BF16)

    def inside(f, r, lone, edge):
        top = jnp.logical_or(r > 0, z > 0)
        low = jnp.logical_or(r < rows + 1, z < nz - 1)
        return jnp.logical_and(jnp.logical_or(lone, edge), jnp.logical_and(top, low))

    def activate(i):
        f, r = lax.div(i, rows + 2), lax.rem(i, rows + 2)
        zz = (L[f, r].astype(F32) - mean) * scale + bias
        v = zz / (1.0 + jnp.exp(-zz))
        keep = inside(f, r, f >= frames, t > 0)
        store_shifts(A, f, r, jnp.where(keep, v, 0.0))

    loop(0, 2 * frames * (rows + 2), activate)

    size = frames * rows * width

    def piece(buf, u):
        kt, kr = lax.div(u, 3), lax.rem(u, 3)
        return buf[pl.ds(kt, frames), pl.ds(kr, rows)].reshape(size, 3 * ch)

    def conv(buf, w):
        def frame_tap(kt):
            left = jnp.concatenate([piece(buf, 3 * kt + kr) for kr in range(3)], axis=1)
            right = w[pl.ds(3 * kt, 3)].reshape(9 * ch, ch)
            return jnp.dot(left, right, preferred_element_type=F32)

        acc[...] = frame_tap(0)

        def more(kt):
            acc[...] += frame_tap(kt)

        loop(1, 3, more)

    conv(A, W)
    target_in.wait()

    def finish(i):
        f, r = lax.div(i, rows), lax.rem(i, rows)
        at_row = pl.ds(pl.multiple_of(i * width, 16), width)
        out = latent[f, r].astype(F32) + acc[at_row, :]
        decoded[f, r] = out.astype(BF16)
        g = out - target[f, r].astype(F32)
        g32[at_row, :] = g
        graw[f, 1 + r] = g.astype(BF16)

    loop(0, frames * rows, finish)

    own = graw.at[pl.ds(0, frames), pl.ds(1, rows)]
    g_halo = halo(own, graw, 0, frames, dn_t, gh_s, gh_r)
    for c in g_halo:
        c.start()
    decoded_out = pltpu.make_async_copy(decoded, decoded_hbm, out_sem.at[0])
    decoded_out.start()

    per = ch // (nx * nz)
    half = ch // 2
    for b in range(ch // 128):
        for q in range(size // 128):
            cols = slice(q * 128, (q + 1) * 128)
            block = g32[cols, b * 128 : (b + 1) * 128].T
            gtb[b * 128 : (b + 1) * 128, cols] = block
            for i in range(128 // per):
                zz, cc = divmod(b * (128 // per) + i, nx)
                gta[(cc * nz + zz) * per : (cc * nz + zz + 1) * per, cols] = (
                    block[i * per : (i + 1) * per]
                )

    def core_p(u):
        return remote(DP.at[other, u], CP.at[u], co_s.at[u], co_r.at[u], at(y, x, other), z)

    def core_z():
        return remote(DZ.at[other], CZ, co_s.at[8], co_r.at[8], at(y, x, other), z)

    gta16[...] = gta[...].astype(BF16)
    gtb16[...] = gtb[...].astype(BF16)

    def kernel_term(gt, unit, store):
        res = jnp.dot(gt[...], piece(A, unit), preferred_element_type=F32)
        for kc in range(3):
            for h in range(2):
                lo = kc * ch + h * half
                store(h, kc, res[:, lo : lo + half])

    def term_p(u):
        def store(h, kc, v):
            DP[h, u, :, :, kc] = v.reshape(nx, nz, per, half)

        kernel_term(gta16, u, store)
        core_p(u).start()

    def term_z():
        def store(h, kc, v):
            DZ[h, :, :, kc] = v.reshape(nz, nx, per, half)

        kernel_term(gtb16, 8, store)
        core_z().start()

    def along(u, d):
        s = lax.div(u, 4)
        xx = lax.rem(x + (1 - s) * d + nx, nx)
        yy = lax.rem(y + s * d + ny, ny)
        return x * (1 - s) + y * s, at(yy, xx, core)

    def ring_p(u, step):
        me, up = along(u, 1)
        _, down = along(u, -1)
        sems = [(p_s.at[u, step, d], p_r.at[u, step, d]) for d in range(2)]
        if step == 0:
            far = DP.at[core, u, lax.rem(me + 2, 4)]
            return [
                remote(far.at[pl.ds(0, nz // 2)], PH.at[u, 0], *sems[0], up, z),
                remote(far.at[pl.ds(nz // 2, nz // 2)], PH.at[u, 1], *sems[1], down, z),
            ]
        return [
            remote(DP.at[core, u, lax.rem(me + 1, 4)], PF.at[u, 0], *sems[0], up, z),
            remote(DP.at[core, u, lax.rem(me + 3, 4)], PF.at[u, 1], *sems[1], down, z),
        ]

    def recv_p(u, step):
        me, _ = along(u, 1)
        for c in ring_p(u, step):
            c.wait_recv()
        if step == 0:
            right, left = lax.rem(me + 1, 4), lax.rem(me + 3, 4)
            h = nz // 2
            DP[core, u, right, 0:h] = DP[core, u, right, 0:h] + PH[u, 0]
            DP[core, u, left, h:nz] = DP[core, u, left, h:nz] + PH[u, 1]
        else:
            DP[core, u, me] = DP[core, u, me] + PF[u, 0] + PF[u, 1]

    def order(i):
        return lax.rem(i, 2) * 4 + lax.div(i, 2)

    def first_p(u):
        core_p(u).wait_recv()
        DP[core, u] = DP[core, u] + CP[u]
        for c in ring_p(u, 0):
            c.start()

    sz = nz // 2

    def ring_z(step):
        sems = [(z_s.at[step, d], z_r.at[step, d]) for d in range(2)]
        if step == 0:
            far = DZ.at[core, lax.rem(z + sz, nz)]
            return [
                remote(far.at[pl.ds(0, nx // 2)], ZH.at[0], *sems[0], t, up_z),
                remote(far.at[pl.ds(nx // 2, nx // 2)], ZH.at[1], *sems[1], t, dn_z),
            ]
        up, down = lax.rem(z + sz - step, nz), lax.rem(z + nz - sz + step, nz)
        return [
            remote(DZ.at[core, up], ZF.at[step - 1, 0], *sems[0], t, up_z),
            remote(DZ.at[core, down], ZF.at[step - 1, 1], *sems[1], t, dn_z),
        ]

    def recv_z(step):
        for c in ring_z(step):
            c.wait_recv()
        left = lax.rem(z + nz - 1 + sz - step, nz)
        right = lax.rem(z + nz + 1 - sz + step, nz)
        if step == 0:
            h = nx // 2
            DZ[core, left, 0:h] = DZ[core, left, 0:h] + ZH[0]
            DZ[core, right, h:nx] = DZ[core, right, h:nx] + ZH[1]
        else:
            DZ[core, left] = DZ[core, left] + ZF[step - 1, 0]
            DZ[core, right] = DZ[core, right] + ZF[step - 1, 1]
        if step + 1 < sz:
            for c in ring_z(step + 1):
                c.start()

    def wave_0(i):
        u = order(i)
        recv_p(u, 0)
        for c in ring_p(u, 1):
            c.start()

    term_z()
    term_p(order(0))
    term_p(order(1))
    core_z().wait_recv()
    DZ[core] = DZ[core] + CZ[...]
    for c in ring_z(0):
        c.start()

    def term_2(i):
        term_p(order(i))
        first_p(order(i - 2))

    def term_3(i):
        term_2(i)
        wave_0(i - 5)

    loop(2, 5, term_2)
    recv_z(0)
    loop(5, 8, term_3)
    first_p(order(6))
    first_p(order(7))
    loop(3, 6, wave_0)
    recv_z(1)
    loop(6, 8, wave_0)

    def cross(s, k):
        yy = lax.rem(y + (1 - s) * k, ny)
        xx = lax.rem(x + s * k, nx)
        me = x * (1 - s) + y * s
        u = 4 * s + yy * (1 - s) + xx * s
        return remote(
            DP.at[core, u, me], Q2.at[s, k], q_s.at[s, k], q_r.at[s, k], at(yy, xx, core), z
        )

    def wave_1(i):
        u = order(i)
        recv_p(u, 1)
        s, v = lax.div(u, 4), lax.rem(u, 4)
        here = y * (1 - s) + x * s

        @pl.when(v != here)
        def _():
            cross(s, lax.rem(v - here + 4, 4)).start()

    def sum_z(k):
        c = lax.rem(z + k, nz)
        return remote(Q.at[c], Q3.at[k], q3_s.at[k], q3_r.at[k], t, c)

    def wave_2():
        for s in range(2):
            loop(1, 4, lambda k: cross(s, k).wait_recv())
            me, here = (x, y) if s == 0 else (y, x)
            Q[:, s] = DP[core, 4 * s + here, me] + Q2[s, 1] + Q2[s, 2] + Q2[s, 3]
        for k in (4, 3, 5, 2, 6, 1, 7):
            sum_z(k).start()

    def z_to_x(k):
        xx = lax.rem(x + k, nx)
        return remote(
            DZ.at[core, z, xx], ZX.at[k], zx_s.at[k], zx_r.at[k], at(y, xx, core), z
        )

    me_xy = y * nx + x

    def publish(k):
        p = lax.rem(me_xy + k, n2)
        slot = XG.at[me_xy, core]
        return remote(slot, slot, xg_s.at[k], xg_r.at[k], p * 2 + core, z)

    def to_core(k):
        slot = XG.at[lax.rem(me_xy + n2 - k, n2), core]
        return remote(slot, slot, cg_s.at[k], cg_r.at[k], at(y, x, other), z)

    def publish_z(k):
        p = lax.rem(me_xy + k, n2)
        slot = XZ.at[me_xy, core]
        return remote(slot, slot, xz_s.at[k], xz_r.at[k], p * 2 + core, z)

    def to_core_z():
        slot = XZ.at[:, core]
        return remote(slot, slot, cz_s.at[0], cz_r.at[0], at(y, x, other), z)

    def finish_z():
        loop(1, nx, lambda k: z_to_x(k).wait_recv())
        total = DZ[core, z, x]
        for k in range(1, nx):
            total = total + ZX[k]
        XZ[me_xy, core] = total
        for k in FAR_FIRST[1]:
            publish_z(k).start()

    def wave_3():
        loop(1, nz, lambda k: sum_z(k).wait_recv())
        total = Q[z]
        for k in range(1, nz):
            total = total + Q3[k]
        XG[me_xy, core] = total
        for k in FAR_FIRST[1]:
            publish(k).start()
        to_core(0).start()
        loop(1, n2, lambda k: publish_z(k).wait_recv())
        to_core_z().start()

    for c in g_halo:
        c.wait()

    def shift_gradient(i):
        f, r = lax.div(i, rows + 2), lax.rem(i, rows + 2)
        keep = inside(f, r, f < frames, t < nt - 1)
        store_shifts(G, f, r, jnp.where(keep, graw[f, r].astype(F32), 0.0))

    loop(0, 2 * frames * (rows + 2), shift_gradient)
    recv_z(2)
    conv(G, WT)
    recv_z(3)
    loop(1, nx, lambda k: z_to_x(k).start())

    def through_norm(i, carry):
        s0, s1 = carry
        f, r = lax.div(i, rows), lax.rem(i, rows)
        at_row = pl.ds(pl.multiple_of(i * width, 16), width)
        d = latent[f, r].astype(F32) - mean
        zz = d * scale + bias
        sig = 1.0 / (1.0 + jnp.exp(-zz))
        gz = acc[at_row, :] * sig * (1.0 + zz * (1.0 - sig))
        acc[at_row, :] = gz
        return s0 + eights(gz), s1 + eights(gz * (d * rstd))

    zero = jnp.zeros((8, ch), F32)
    s0, s1 = lax.fori_loop(0, frames * rows, through_norm, (zero, zero))
    spread_out(2, pack(jnp.sum(s0, axis=0, keepdims=True), jnp.sum(s1, axis=0, keepdims=True)))
    loop(0, 8, wave_1)
    finish_z()
    n = gather_in(2)
    spread_out(3, plain_total(2, n))
    wave_2()
    n = gather_in(3)
    s0, s1 = unpack(plain_total(3, n))
    bgrad[...] = s0
    ngrad[...] = s1
    m1 = group_sum(s0 * gain) / everything
    m2 = group_sum(s1 * gain) / everything

    def to_input(i):
        f, r = lax.div(i, rows), lax.rem(i, rows)
        at_row = pl.ds(pl.multiple_of(i * width, 16), width)
        xhat = (latent[f, r].astype(F32) - mean) * rstd
        gx = acc[at_row, :] * gain
        grad_latent[f, r] = (g32[at_row, :] + rstd * (gx - m1 - xhat * m2)).astype(BF16)

    loop(0, frames * rows, to_input)
    outs = [
        decoded_out,
        pltpu.make_async_copy(grad_latent, grad_latent_hbm, out_sem.at[1]),
        pltpu.make_async_copy(ngrad, ngrad_hbm, out_sem.at[2]),
        pltpu.make_async_copy(bgrad, bgrad_hbm, out_sem.at[3]),
        pltpu.make_async_copy(wgrad, wgrad_hbm, out_sem.at[4]),
    ]
    for c in outs[1:4]:
        c.start()

    wave_3()

    def pass_on(k):
        publish(k).wait_recv()
        to_core(k).start()

    for k in (12, 4, 1, 3, 15, 13, 7, 5, 8, 2, 11, 9, 14, 6, 10):
        pass_on(k)
    to_core_z().wait_recv()
    loop(0, n2, lambda k: to_core(k).wait_recv())
    for cc in range(2):
        lanes = slice(cc * half, (cc + 1) * half)
        for xx in range(nx):
            for yy in range(ny):
                p = yy * nx + xx
                wgrad[yy, :, xx * per : (xx + 1) * per, lanes] = XG[p, cc, 0]
                wgrad[4 + xx, :, yy * per : (yy + 1) * per, lanes] = XG[p, cc, 1]
            total = XZ[xx, cc]
            for yy in range(1, ny):
                total = total + XZ[yy * nx + xx, cc]
            wgrad[8, :, xx * per : (xx + 1) * per, lanes] = total
    outs[4].start()

    def drain(u):
        core_p(u).wait_send()
        for step in range(2):
            for c in ring_p(u, step):
                c.wait_send()

    loop(0, 8, drain)
    core_z().wait_send()
    for step in range(sz):
        for c in ring_z(step):
            c.wait_send()

    def drain_cross(k):
        cross(0, k).wait_send()
        cross(1, k).wait_send()
        z_to_x(k).wait_send()

    loop(1, 4, drain_cross)
    loop(1, nz, lambda k: sum_z(k).wait_send())
    loop(1, n2, lambda k: publish(k).wait_send())
    loop(1, n2, lambda k: publish_z(k).wait_send())
    to_core_z().wait_send()
    loop(0, n2, lambda k: to_core(k).wait_send())
    for c in outs:
        c.wait()


def hand_over(*refs):
    n = len(refs) // 3
    given, out, held, sem = refs[:n], refs[n : 2 * n], refs[2 * n : 3 * n], refs[-1]
    into = [pltpu.make_async_copy(given[i], held[i], sem.at[0, i]) for i in range(n)]
    onto = [pltpu.make_async_copy(held[i], out[i], sem.at[1, i]) for i in range(n)]
    for c in into:
        c.start()
    for a, b in zip(into, onto):
        a.wait()
        b.start()
    for c in onto:
        c.wait()


def per_device(nx, ny, nz, latent, target, conv_weight, gain, bias):
    frames, rows, width, ch = latent.shape
    size = frames * rows * width
    per, half = ch // (nx * nz), ch // 2
    sz, n2 = nz // 2, nx * ny
    tile = (3, per, half)
    V, D = pltpu.VMEM, pltpu.SemaphoreType.DMA
    padded = (2 * frames, rows + 2, width)
    block = (frames, rows, width, ch)
    most = max(2 * nz, n2)
    scratch = [
        V(padded + (ch,), BF16),
        V(padded + (3 * ch,), BF16),
        V(padded + (3 * ch,), BF16),
        V(padded + (ch,), BF16),
        V((size, ch), F32),
        V((size, ch), F32),
        V((TAPS, 3 * ch, ch), BF16),
        V((TAPS, 3 * ch, ch), BF16),
        V(block, BF16),
        V((1, ch), F32),
        V((1, ch), F32),
        V(block, BF16),
        V(block, BF16),
        V((TAPS, 3, ch // nz, ch), F32),
        V((1, ch), F32),
        V((1, ch), F32),
        V((ch, size), F32),
        V((ch, size), F32),
        V((ch, size), BF16),
        V((ch, size), BF16),
        V((2, 8, nx, nz) + tile, F32),
        V((2, nz, nx) + tile, F32),
        V((8, nx, nz) + tile, F32),
        V((nz, nx) + tile, F32),
        V((8, 2, nz // 2) + tile, F32),
        V((8, 2, nz) + tile, F32),
        V((2, nx // 2) + tile, F32),
        V((max(sz - 1, 1), 2, nx) + tile, F32),
        V((2, 4, nz) + tile, F32),
        V((nz, 2) + tile, F32),
        V((nz, 2) + tile, F32),
        V((nx,) + tile, F32),
        V((n2, 2, 2) + tile, F32),
        V((n2, 2) + tile, F32),
        V((4, most, 8, half), F32),
        D((5,)), D((5,)),
        D((5,)), D((5,)), D((5,)), D((5,)),
        D((4, most)), D((4, most)),
        D((9,)), D((9,)),
        D((8, 2, 2)), D((8, 2, 2)),
        D((sz, 2)), D((sz, 2)),
        D((2, 4)), D((2, 4)),
        D((nz,)), D((nz,)),
        D((nx,)), D((nx,)),
        D((n2,)), D((n2,)), D((n2,)), D((n2,)),
        D((n2,)), D((n2,)), D((1,)), D((1,)),
    ]
    anywhere = pl.BlockSpec(memory_space=pl.ANY)
    shapes = [
        jax.ShapeDtypeStruct(latent.shape, BF16),
        jax.ShapeDtypeStruct(latent.shape, BF16),
        jax.ShapeDtypeStruct((TAPS, 3, ch // nz, ch), F32),
        jax.ShapeDtypeStruct((1, ch), F32),
        jax.ShapeDtypeStruct((1, ch), F32),
    ]
    results = pl.pallas_call(
        functools.partial(kernel, nx, ny, nz, latent.shape),
        out_shape=shapes,
        in_specs=[anywhere] * 5,
        out_specs=[anywhere] * 5,
        scratch_shapes=scratch,
        compiler_params=pltpu.CompilerParams(
            collective_id=0, has_side_effects=True, vmem_limit_bytes=60 * 2**20
        ),
        name="block",
    )(
        latent,
        target,
        conv_weight.reshape(TAPS, 3 * ch, ch),
        gain.reshape(1, ch),
        bias.reshape(1, ch),
    )
    decoded, grad_latent, wgrad, ngrad, bgrad = pl.pallas_call(
        hand_over,
        out_shape=shapes,
        in_specs=[anywhere] * 5,
        out_specs=[anywhere] * 5,
        scratch_shapes=[V(o.shape, o.dtype) for o in shapes] + [D((2, 5))],
        name="hand_over",
    )(*results)
    wgrad = jnp.swapaxes(wgrad.reshape(3, 3, 3, ch // nz, ch), 3, 4)
    return decoded, grad_latent, wgrad, ngrad.reshape(ch), bgrad.reshape(ch)


def solution(mesh, nx=4):
    nt, nz = mesh.shape["tm"], mesh.shape["height"]
    ny = nt // (2 * nx)
    in_specs = (P("tm", "height", None, None), P("tm", "height", None, None), P(), P(), P())
    out_specs = (
        P("tm", "height", None, None),
        P("tm", "height", None, None),
        P(None, None, None, None, "height"),
        P(),
        P(),
    )
    return jax.shard_map(
        functools.partial(per_device, nx, ny, nz),
        mesh=mesh,
        in_specs=in_specs,
        out_specs=out_specs,
        check_vma=False,
    )
```

```python
import functools

import jax
import jax.numpy as jnp
from jax import lax
from jax.experimental import pallas as pl
from jax.experimental.pallas import tpu as pltpu
from jax.sharding import PartitionSpec as P

NORM_GROUPS = 32
EPS = 1e-06
MESH = pl.DeviceIdType.MESH
F32 = jnp.float32
BF16 = jnp.bfloat16
TAPS = 9


def group_sum(v):
    lane = lax.broadcasted_iota(jnp.int32, v.shape, 1)
    width = v.shape[1]
    for k in (1, 2, 4):
        other = jnp.where(
            (lane & k) != 0,
            pltpu.roll(v, k, 1),
            pltpu.roll(v, width - k, 1),
        )
        v = v + other
    return v


def pack(a, b):
    half = a.shape[1] // 2
    return jnp.concatenate(
        [a[:, :half], a[:, half:], b[:, :half], b[:, half:], jnp.zeros((4, half), F32)], axis=0
    )


def unpack(v):
    a = jnp.concatenate([v[0:1], v[1:2]], axis=1)
    b = jnp.concatenate([v[2:3], v[3:4]], axis=1)
    return a, b


FAR_FIRST = (
    (4, 12, 3, 5, 11, 13, 2, 6, 10, 14, 1, 7, 9, 15, 8),
    (10, 6, 14, 9, 11, 2, 8, 5, 7, 13, 15, 3, 1, 4, 12),
)


def kernel(
    nx, ny, nz, shape,
    latent_hbm, target_hbm, w_hbm, gain_hbm, bias_hbm,
    decoded, grad_latent, wgrad, ngrad, bgrad,
    L, A, G, graw, g32, acc, W, WT, target, gain_ref, bias_ref,
    gta, gtb, gta16, gtb16, DP, DZ, CP, CZ,
    PX, PY, PF, ZH, ZF, Q2, Q, Q3, ZX, XG, XZ, AR,
    in_sem, lat_s, lat_r, gh_s, gh_r, ar_s, ar_r, co_s, co_r,
    p_s, p_r, z_s, z_r, q_s, q_r, q3_s, q3_r, zx_s, zx_r, xg_s, xg_r, cg_s, cg_r,
    xz_s, xz_r, cz_s, cz_r,
):
    t = lax.axis_index("tm")
    z = lax.axis_index("height")
    nt = 2 * nx * ny
    core = lax.rem(t, 2)
    x = lax.rem(lax.div(t, 2), nx)
    y = lax.div(t, 2 * nx)
    frames, rows, width, ch = shape
    other = 1 - core

    def at(yy, xx, cc):
        return (yy * nx + xx) * 2 + cc

    def remote(src, dst, ss, rs, tt, zz):
        return pltpu.make_async_remote_copy(
            src_ref=src, dst_ref=dst, send_sem=ss, recv_sem=rs,
            device_id=(tt, zz), device_id_type=MESH,
        )

    def loop(lo, hi, f):
        def step(i, c):
            f(i)
            return c

        lax.fori_loop(lo, hi, step, 0)

    up_t, dn_t = lax.rem(t + 1, nt), lax.rem(t + nt - 1, nt)
    up_z, dn_z = lax.rem(z + 1, nz), lax.rem(z + nz - 1, nz)

    latent = L.at[pl.ds(frames, frames), pl.ds(1, rows)]
    latent_in = pltpu.make_async_copy(latent_hbm, latent, in_sem.at[0])
    latent_in.start()

    n1, n2 = 2 * nz, nx * ny
    me1, me2 = core * nz + z, y * nx + x

    def peer1(k):
        p = lax.rem(me1 + k, n1)
        return at(y, x, lax.div(p, nz)), lax.rem(p, nz)

    def peer2(k):
        p = lax.rem(me2 + k, n2)
        return p * 2 + core, z

    barrier = pltpu.get_barrier_semaphore()

    def greet(tt, zz):
        pl.semaphore_signal(barrier, inc=1, device_id=(tt, zz), device_id_type=MESH)

    loop(1, n1, lambda k: greet(*peer1(k)))
    loop(1, n2, lambda k: greet(*peer2(k)))
    for tt in (up_t, dn_t):
        for zz in (dn_z, z, up_z):
            greet(tt, zz)

    gain_in = pltpu.make_async_copy(gain_hbm, gain_ref, in_sem.at[1])
    bias_in = pltpu.make_async_copy(bias_hbm, bias_ref, in_sem.at[2])
    weights_in = pltpu.make_async_copy(w_hbm, W, in_sem.at[3])
    target_in = pltpu.make_async_copy(target_hbm, target, in_sem.at[4])
    for c in (gain_in, bias_in, weights_in, target_in):
        c.start()
    latent_in.wait()

    def eights(v):
        return jnp.sum(v.reshape(width // 8, 8, ch), axis=0)

    def sum_rows(i, total):
        return total + eights(latent[lax.div(i, rows), lax.rem(i, rows)].astype(F32))

    count = frames * rows * width * 8
    total = lax.fori_loop(0, frames * rows, sum_rows, jnp.zeros((8, ch), F32))
    mean_l = group_sum(jnp.sum(total, axis=0, keepdims=True)) / count

    def sum_squares(i, total):
        v = latent[lax.div(i, rows), lax.rem(i, rows)].astype(F32) - mean_l
        return total + eights(v * v)

    total = lax.fori_loop(0, frames * rows, sum_squares, jnp.zeros((8, ch), F32))
    sq_l = group_sum(jnp.sum(total, axis=0, keepdims=True))

    pl.semaphore_wait(barrier, (n1 - 1) + (n2 - 1) + 6)

    def exchange(stage, k):
        me, peer = (me1, peer1) if stage % 2 == 0 else (me2, peer2)
        slot = AR.at[stage, me]
        return remote(slot, slot, ar_s.at[stage, k], ar_r.at[stage, k], *peer(k))

    def spread_out(stage, value):
        me, n = (me1, n1) if stage % 2 == 0 else (me2, n2)
        AR[stage, me] = value
        for k in FAR_FIRST[stage % 2]:
            if k < n:
                exchange(stage, k).start()

    def gather_in(stage):
        n = n1 if stage % 2 == 0 else n2
        loop(1, n, lambda k: exchange(stage, k).wait())
        return n

    def plain_total(stage, n):
        total = AR[stage, 0]
        for k in range(1, n):
            total = total + AR[stage, k]
        return total

    def moments(stage, n, members):
        mean = plain_total(stage, n)[0:2] / n
        sq = jnp.zeros_like(mean)
        for k in range(n):
            d = AR[stage, k, 0:2] - mean
            sq = sq + (AR[stage, k, 2:4] + (d * d) * members)
        return jnp.concatenate([mean, sq, jnp.zeros((4, mean.shape[1]), F32)], axis=0)

    spread_out(0, pack(mean_l, sq_l))

    def halo(block, buf, first, away, tt, ss, rs):
        edge0, edge1 = block.at[:, 0], block.at[:, rows - 1]
        mine, theirs = pl.ds(first, frames), pl.ds(away, frames)
        return [
            remote(block, buf.at[theirs, pl.ds(1, rows)], ss.at[0], rs.at[0], tt, z),
            remote(edge1, buf.at[mine, 0], ss.at[1], rs.at[1], t, up_z),
            remote(edge0, buf.at[mine, rows + 1], ss.at[2], rs.at[2], t, dn_z),
            remote(edge1, buf.at[theirs, 0], ss.at[3], rs.at[3], tt, up_z),
            remote(edge0, buf.at[theirs, rows + 1], ss.at[4], rs.at[4], tt, dn_z),
        ]

    lat_halo = halo(latent, L, frames, 0, up_t, lat_s, lat_r)
    for c in lat_halo:
        c.start()

    def flip(u):
        for kc in range(3):
            WT[8 - u, (2 - kc) * ch : (3 - kc) * ch, :] = W[u, kc * ch : (kc + 1) * ch, :].T

    n = gather_in(0)
    spread_out(1, moments(0, n, count))
    weights_in.wait()
    loop(0, TAPS, flip)
    gain_in.wait()
    bias_in.wait()
    n = gather_in(1)
    mean, sq = unpack(moments(1, n, count * n1))
    everything = count * n1 * n2
    rstd = lax.rsqrt(sq / everything + EPS)
    gain, bias = gain_ref[...], bias_ref[...]
    scale = rstd * gain

    for c in lat_halo:
        c.wait()

    col = lax.broadcasted_iota(jnp.int32, (width, ch), 0)

    def store_shifts(buf, f, r, v):
        buf[f, r, :, 0:ch] = jnp.where(col == 0, 0.0, pltpu.roll(v, 1, 0)).astype(BF16)
        buf[f, r, :, ch : 2 * ch] = v.astype(BF16)
        buf[f, r, :, 2 * ch : 3 * ch] = jnp.where(
            col == width - 1, 0.0, pltpu.roll(v, width - 1, 0)
        ).astype(BF16)

    def inside(f, r, lone, edge):
        top = jnp.logical_or(r > 0, z > 0)
        low = jnp.logical_or(r < rows + 1, z < nz - 1)
        return jnp.logical_and(jnp.logical_or(lone, edge), jnp.logical_and(top, low))

    def activate(i):
        f, r = lax.div(i, rows + 2), lax.rem(i, rows + 2)
        zz = (L[f, r].astype(F32) - mean) * scale + bias
        v = zz / (1.0 + jnp.exp(-zz))
        keep = inside(f, r, f >= frames, t > 0)
        store_shifts(A, f, r, jnp.where(keep, v, 0.0))

    loop(0, 2 * frames * (rows + 2), activate)

    size = frames * rows * width

    def piece(buf, u):
        kt, kr = lax.div(u, 3), lax.rem(u, 3)
        return buf[pl.ds(kt, frames), pl.ds(kr, rows)].reshape(size, 3 * ch)

    def conv(buf, w):
        def frame_tap(kt):
            left = jnp.concatenate([piece(buf, 3 * kt + kr) for kr in range(3)], axis=1)
            right = w[pl.ds(3 * kt, 3)].reshape(9 * ch, ch)
            return jnp.dot(left, right, preferred_element_type=F32)

        acc[...] = frame_tap(0)

        def more(kt):
            acc[...] += frame_tap(kt)

        loop(1, 3, more)

    conv(A, W)
    target_in.wait()

    def finish(i):
        f, r = lax.div(i, rows), lax.rem(i, rows)
        at_row = pl.ds(pl.multiple_of(i * width, 16), width)
        out = latent[f, r].astype(F32) + acc[at_row, :]
        decoded[f, r] = out.astype(BF16)
        g = out - target[f, r].astype(F32)
        g32[at_row, :] = g
        graw[f, 1 + r] = g.astype(BF16)

    loop(0, frames * rows, finish)

    own = graw.at[pl.ds(0, frames), pl.ds(1, rows)]
    g_halo = halo(own, graw, 0, frames, dn_t, gh_s, gh_r)
    for c in g_halo:
        c.start()

    per = ch // (nx * nz)
    half = ch // 2
    for b in range(ch // 128):
        for q in range(size // 128):
            cols = slice(q * 128, (q + 1) * 128)
            block = g32[cols, b * 128 : (b + 1) * 128].T
            gtb[b * 128 : (b + 1) * 128, cols] = block
            for i in range(128 // per):
                zz, cc = divmod(b * (128 // per) + i, nx)
                gta[(cc * nz + zz) * per : (cc * nz + zz + 1) * per, cols] = (
                    block[i * per : (i + 1) * per]
                )

    def core_p(u):
        return remote(DP.at[other, u], CP.at[u], co_s.at[u], co_r.at[u], at(y, x, other), z)

    def core_z():
        return remote(DZ.at[other], CZ, co_s.at[8], co_r.at[8], at(y, x, other), z)

    gta16[...] = gta[...].astype(BF16)
    gtb16[...] = gtb[...].astype(BF16)

    def kernel_term(gt, unit, store):
        res = jnp.dot(gt[...], piece(A, unit), preferred_element_type=F32)
        for kc in range(3):
            for h in range(2):
                lo = kc * ch + h * half
                store(h, kc, res[:, lo : lo + half])

    def term_p(u):
        def store(h, kc, v):
            DP[h, u, :, :, kc] = v.reshape(nx, nz, per, half)

        kernel_term(gta16, u, store)
        core_p(u).start()

    def term_z():
        def store(h, kc, v):
            DZ[h, :, :, kc] = v.reshape(nz, nx, per, half)

        kernel_term(gtb16, 8, store)
        core_z().start()

    cuts = (nz * 6 // 8, nz // 2)

    def along(s, d):
        xx = lax.rem(x + (1 - s) * d + nx, nx)
        yy = lax.rem(y + s * d + ny, ny)
        return at(yy, xx, core)

    def ring_p(s, j, step):
        u = 4 * s + j
        me, up, down = (x, y)[s], along(s, 1), along(s, -1)
        sems = [(p_s.at[u, step, d], p_r.at[u, step, d]) for d in range(2)]
        if step == 0:
            far, cut, buf = DP.at[core, u, lax.rem(me + 2, 4)], cuts[s], (PX, PY)[s].at[j]
            head, rest = pl.ds(0, cut), pl.ds(cut, nz - cut)
            return [
                remote(far.at[head], buf.at[head], *sems[0], up, z),
                remote(far.at[rest], buf.at[rest], *sems[1], down, z),
            ]
        return [
            remote(DP.at[core, u, lax.rem(me + 1, 4)], PF.at[u, 0], *sems[0], up, z),
            remote(DP.at[core, u, lax.rem(me + 3, 4)], PF.at[u, 1], *sems[1], down, z),
        ]

    def recv_p(s, j, step):
        u, me = 4 * s + j, (x, y)[s]
        for c in ring_p(s, j, step):
            c.wait_recv()
        if step == 0:
            right, left = lax.rem(me + 1, 4), lax.rem(me + 3, 4)
            cut, buf = cuts[s], (PX, PY)[s]
            DP[core, u, right, 0:cut] = DP[core, u, right, 0:cut] + buf[j, 0:cut]
            DP[core, u, left, cut:nz] = DP[core, u, left, cut:nz] + buf[j, cut:nz]
        else:
            DP[core, u, me] = DP[core, u, me] + PF[u, 0] + PF[u, 1]

    def first_p(s, j):
        u = 4 * s + j
        core_p(u).wait_recv()
        DP[core, u] = DP[core, u] + CP[u]
        for c in ring_p(s, j, 0):
            c.start()

    sz = nz // 2

    def ring_z(step):
        sems = [(z_s.at[step, d], z_r.at[step, d]) for d in range(2)]
        if step == 0:
            far = DZ.at[core, lax.rem(z + sz, nz)]
            return [
                remote(far.at[pl.ds(0, nx // 2)], ZH.at[0], *sems[0], t, up_z),
                remote(far.at[pl.ds(nx // 2, nx // 2)], ZH.at[1], *sems[1], t, dn_z),
            ]
        up, down = lax.rem(z + sz - step, nz), lax.rem(z + nz - sz + step, nz)
        return [
            remote(DZ.at[core, up], ZF.at[step - 1, 0], *sems[0], t, up_z),
            remote(DZ.at[core, down], ZF.at[step - 1, 1], *sems[1], t, dn_z),
        ]

    def recv_z(step):
        for c in ring_z(step):
            c.wait_recv()
        left = lax.rem(z + nz - 1 + sz - step, nz)
        right = lax.rem(z + nz + 1 - sz + step, nz)
        if step == 0:
            h = nx // 2
            DZ[core, left, 0:h] = DZ[core, left, 0:h] + ZH[0]
            DZ[core, right, h:nx] = DZ[core, right, h:nx] + ZH[1]
        else:
            DZ[core, left] = DZ[core, left] + ZF[step - 1, 0]
            DZ[core, right] = DZ[core, right] + ZF[step - 1, 1]
        if step + 1 < sz:
            for c in ring_z(step + 1):
                c.start()

    def wave_0(j):
        for s in range(2):
            recv_p(s, j, 0)
            for c in ring_p(s, j, 1):
                c.start()

    def terms(j):
        for s in range(2):
            term_p(4 * s + j)

    def terms_and_first(j):
        for s in range(2):
            term_p(4 * s + j)
            first_p(s, j - 2)

    def first_z():
        core_z().wait_recv()
        DZ[core] = DZ[core] + CZ[...]
        for c in ring_z(0):
            c.start()

    def firsts(j):
        for s in range(2):
            first_p(s, j)

    term_z()
    loop(0, 2, terms)
    first_z()
    loop(2, 4, terms_and_first)
    loop(4 - 2, 4, firsts)
    loop(0, 2, wave_0)
    recv_z(0)
    loop(2, 4, wave_0)
    recv_z(1)

    def cross(s, k):
        yy = lax.rem(y + (1 - s) * k, ny)
        xx = lax.rem(x + s * k, nx)
        me = x * (1 - s) + y * s
        u = 4 * s + yy * (1 - s) + xx * s
        return remote(
            DP.at[core, u, me], Q2.at[s, k], q_s.at[s, k], q_r.at[s, k], at(yy, xx, core), z
        )

    def wave_1(j):
        for s in range(2):
            recv_p(s, j, 1)
            here = (y, x)[s]

            @pl.when(j != here)
            def _():
                cross(s, lax.rem(j - here + 4, 4)).start()

    def sum_z(k):
        c = lax.rem(z + k, nz)
        return remote(Q.at[c], Q3.at[k], q3_s.at[k], q3_r.at[k], t, c)

    def wave_2():
        for s in range(2):
            loop(1, 4, lambda k: cross(s, k).wait_recv())
            me, here = (x, y) if s == 0 else (y, x)
            Q[:, s] = DP[core, 4 * s + here, me] + Q2[s, 1] + Q2[s, 2] + Q2[s, 3]
        for k in (4, 3, 5, 2, 6, 1, 7):
            sum_z(k).start()

    def z_to_x(k):
        xx = lax.rem(x + k, nx)
        return remote(
            DZ.at[core, z, xx], ZX.at[k], zx_s.at[k], zx_r.at[k], at(y, xx, core), z
        )

    me_xy = y * nx + x

    def publish(k):
        p = lax.rem(me_xy + k, n2)
        slot = XG.at[me_xy, core]
        return remote(slot, slot, xg_s.at[k], xg_r.at[k], p * 2 + core, z)

    def to_core(k):
        slot = XG.at[lax.rem(me_xy + n2 - k, n2), core]
        return remote(slot, slot, cg_s.at[k], cg_r.at[k], at(y, x, other), z)

    def publish_z(k):
        p = lax.rem(me_xy + k, n2)
        slot = XZ.at[me_xy, core]
        return remote(slot, slot, xz_s.at[k], xz_r.at[k], p * 2 + core, z)

    def to_core_z():
        slot = XZ.at[:, core]
        return remote(slot, slot, cz_s.at[0], cz_r.at[0], at(y, x, other), z)

    def finish_z():
        loop(1, nx, lambda k: z_to_x(k).wait_recv())
        total = DZ[core, z, x]
        for k in range(1, nx):
            total = total + ZX[k]
        XZ[me_xy, core] = total
        for k in FAR_FIRST[1]:
            publish_z(k).start()

    def wave_3():
        loop(1, nz, lambda k: sum_z(k).wait_recv())
        total = Q[z]
        for k in range(1, nz):
            total = total + Q3[k]
        XG[me_xy, core] = total
        for k in FAR_FIRST[1]:
            publish(k).start()
        to_core(0).start()
        loop(1, n2, lambda k: publish_z(k).wait_recv())
        to_core_z().start()

    for c in g_halo:
        c.wait()

    def shift_gradient(i):
        f, r = lax.div(i, rows + 2), lax.rem(i, rows + 2)
        keep = inside(f, r, f < frames, t < nt - 1)
        store_shifts(G, f, r, jnp.where(keep, graw[f, r].astype(F32), 0.0))

    loop(0, 2 * frames * (rows + 2), shift_gradient)
    recv_z(2)
    conv(G, WT)
    recv_z(3)
    loop(1, nx, lambda k: z_to_x(k).start())

    def through_norm(i, carry):
        s0, s1 = carry
        f, r = lax.div(i, rows), lax.rem(i, rows)
        at_row = pl.ds(pl.multiple_of(i * width, 16), width)
        d = latent[f, r].astype(F32) - mean
        zz = d * scale + bias
        sig = 1.0 / (1.0 + jnp.exp(-zz))
        gz = acc[at_row, :] * sig * (1.0 + zz * (1.0 - sig))
        acc[at_row, :] = gz
        return s0 + eights(gz), s1 + eights(gz * (d * rstd))

    zero = jnp.zeros((8, ch), F32)
    s0, s1 = lax.fori_loop(0, frames * rows, through_norm, (zero, zero))
    spread_out(2, pack(jnp.sum(s0, axis=0, keepdims=True), jnp.sum(s1, axis=0, keepdims=True)))
    loop(0, 4, wave_1)
    finish_z()
    n = gather_in(2)
    spread_out(3, plain_total(2, n))
    wave_2()
    n = gather_in(3)
    s0, s1 = unpack(plain_total(3, n))
    bgrad[...] = s0
    ngrad[...] = s1
    m1 = group_sum(s0 * gain) / everything
    m2 = group_sum(s1 * gain) / everything

    def to_input(i):
        f, r = lax.div(i, rows), lax.rem(i, rows)
        at_row = pl.ds(pl.multiple_of(i * width, 16), width)
        xhat = (latent[f, r].astype(F32) - mean) * rstd
        gx = acc[at_row, :] * gain
        grad_latent[f, r] = (g32[at_row, :] + rstd * (gx - m1 - xhat * m2)).astype(BF16)

    loop(0, frames * rows, to_input)

    wave_3()

    def pass_on(k):
        publish(k).wait_recv()
        to_core(k).start()

    for k in (12, 4, 1, 3, 15, 13, 7, 5, 8, 2, 11, 9, 14, 6, 10):
        pass_on(k)
    to_core_z().wait_recv()
    loop(0, n2, lambda k: to_core(k).wait_recv())
    for cc in range(2):
        lanes = slice(cc * half, (cc + 1) * half)
        for xx in range(nx):
            for yy in range(ny):
                p = yy * nx + xx
                wgrad[yy, :, xx * per : (xx + 1) * per, lanes] = XG[p, cc, 0]
                wgrad[4 + xx, :, yy * per : (yy + 1) * per, lanes] = XG[p, cc, 1]
            total = XZ[xx, cc]
            for yy in range(1, ny):
                total = total + XZ[yy * nx + xx, cc]
            wgrad[8, :, xx * per : (xx + 1) * per, lanes] = total

    def drain(j):
        for s in range(2):
            core_p(4 * s + j).wait_send()
            for step in range(2):
                for c in ring_p(s, j, step):
                    c.wait_send()

    loop(0, 4, drain)
    core_z().wait_send()
    for step in range(sz):
        for c in ring_z(step):
            c.wait_send()

    def drain_cross(k):
        cross(0, k).wait_send()
        cross(1, k).wait_send()
        z_to_x(k).wait_send()

    loop(1, 4, drain_cross)
    loop(1, nz, lambda k: sum_z(k).wait_send())
    loop(1, n2, lambda k: publish(k).wait_send())
    loop(1, n2, lambda k: publish_z(k).wait_send())
    to_core_z().wait_send()
    loop(0, n2, lambda k: to_core(k).wait_send())


def hand_over(*refs):
    n = len(refs) // 2
    copies = [pltpu.make_async_copy(refs[i], refs[n + i], refs[-1].at[i]) for i in range(n)]
    for c in copies:
        c.start()
    for c in copies:
        c.wait()


def per_device(nx, ny, nz, latent, target, conv_weight, gain, bias):
    frames, rows, width, ch = latent.shape
    size = frames * rows * width
    per, half = ch // (nx * nz), ch // 2
    sz, n2 = nz // 2, nx * ny
    tile = (3, per, half)
    V, D = pltpu.VMEM, pltpu.SemaphoreType.DMA
    padded = (2 * frames, rows + 2, width)
    block = (frames, rows, width, ch)
    most = max(2 * nz, n2)
    scratch = [
        V(padded + (ch,), BF16),
        V(padded + (3 * ch,), BF16),
        V(padded + (3 * ch,), BF16),
        V(padded + (ch,), BF16),
        V((size, ch), F32),
        V((size, ch), F32),
        V((TAPS, 3 * ch, ch), BF16),
        V((TAPS, 3 * ch, ch), BF16),
        V(block, BF16),
        V((1, ch), F32),
        V((1, ch), F32),
        V((ch, size), F32),
        V((ch, size), F32),
        V((ch, size), BF16),
        V((ch, size), BF16),
        V((2, 8, nx, nz) + tile, F32),
        V((2, nz, nx) + tile, F32),
        V((8, nx, nz) + tile, F32),
        V((nz, nx) + tile, F32),
        V((4, nz) + tile, F32),
        V((4, nz) + tile, F32),
        V((8, 2, nz) + tile, F32),
        V((2, nx // 2) + tile, F32),
        V((max(sz - 1, 1), 2, nx) + tile, F32),
        V((2, 4, nz) + tile, F32),
        V((nz, 2) + tile, F32),
        V((nz, 2) + tile, F32),
        V((nx,) + tile, F32),
        V((n2, 2, 2) + tile, F32),
        V((n2, 2) + tile, F32),
        V((4, most, 8, half), F32),
        D((5,)),
        D((5,)), D((5,)), D((5,)), D((5,)),
        D((4, most)), D((4, most)),
        D((9,)), D((9,)),
        D((8, 2, 2)), D((8, 2, 2)),
        D((sz, 2)), D((sz, 2)),
        D((2, 4)), D((2, 4)),
        D((nz,)), D((nz,)),
        D((nx,)), D((nx,)),
        D((n2,)), D((n2,)), D((n2,)), D((n2,)),
        D((n2,)), D((n2,)), D((1,)), D((1,)),
    ]
    anywhere = pl.BlockSpec(memory_space=pl.ANY)
    shapes = [
        jax.ShapeDtypeStruct(latent.shape, BF16),
        jax.ShapeDtypeStruct(latent.shape, BF16),
        jax.ShapeDtypeStruct((TAPS, 3, ch // nz, ch), F32),
        jax.ShapeDtypeStruct((1, ch), F32),
        jax.ShapeDtypeStruct((1, ch), F32),
    ]
    results = pl.pallas_call(
        functools.partial(kernel, nx, ny, nz, latent.shape),
        out_shape=[V(o.shape, o.dtype) for o in shapes],
        in_specs=[pl.BlockSpec(memory_space=pltpu.HBM)] * 5,
        out_specs=[pl.BlockSpec(memory_space=V)] * 5,
        scratch_shapes=scratch,
        compiler_params=pltpu.CompilerParams(
            collective_id=0, has_side_effects=True, vmem_limit_bytes=52 * 2**20
        ),
        name="block",
    )(
        *(
            pltpu.with_memory_space_constraint(v, pltpu.HBM)
            for v in (
                latent,
                target,
                conv_weight.reshape(TAPS, 3 * ch, ch),
                gain.reshape(1, ch),
                bias.reshape(1, ch),
            )
        )
    )
    decoded, grad_latent, wgrad, ngrad, bgrad = pl.pallas_call(
        hand_over,
        out_shape=shapes,
        in_specs=[anywhere] * 5,
        out_specs=[anywhere] * 5,
        scratch_shapes=[D((5,))],
        name="hand_over",
    )(*(pltpu.with_memory_space_constraint(r, V) for r in results))
    wgrad = jnp.swapaxes(wgrad.reshape(3, 3, 3, ch // nz, ch), 3, 4)
    return decoded, grad_latent, wgrad, ngrad.reshape(ch), bgrad.reshape(ch)


def solution(mesh, nx=4):
    nt, nz = mesh.shape["tm"], mesh.shape["height"]
    ny = nt // (2 * nx)
    in_specs = (P("tm", "height", None, None), P("tm", "height", None, None), P(), P(), P())
    out_specs = (
        P("tm", "height", None, None),
        P("tm", "height", None, None),
        P(None, None, None, None, "height"),
        P(),
        P(),
    )
    return jax.shard_map(
        functools.partial(per_device, nx, ny, nz),
        mesh=mesh,
        in_specs=in_specs,
        out_specs=out_specs,
        check_vma=False,
    )
```
